32 devices in a mesh: seqs: 4 (over y, x), row: 2 (over core), col: 4 (over z).
Axes of the slice: x: 2, y: 2, z: 4, core: 2. Of those that a mesh axis runs over, the one named last changes fastest.
Arguments:
- tokens: bfloat16 [32, 768, 1024], P('seqs', 'col', 'row'), may hold values from -6 to 6
- lengths: int32 [32], P('seqs'), may hold values from 256 to 1024, as said below
- query_weight: float32 [768, 768], P('row', 'col'), may hold values from -0.21875 to 0.21875
- query_bias: float32 [768], P('col'), may hold values from -3 to 3
- key_weight: float32 [768, 768], P('row', 'col'), may hold values from -0.21875 to 0.21875
- value_weight: float32 [768, 768], P('row', 'col'), may hold values from -0.21875 to 0.21875
- value_bias: float32 [768], P('col'), may hold values from -0.4375 to 0.4375
- out_weight: float32 [768, 768], P('col', 'row'), may hold values from -4 to 4
- out_bias: float32 [768], P('col'), may hold values from -1.5 to 1.5
- first_gain: float32 [768], P('col'), may hold values from 0.5 to 1.5
- first_shift: float32 [768], P('col'), may hold values from -3 to 3
- up_weight: float32 [768, 3072], P('row', 'col'), may hold values from -0.21875 to 0.21875
- up_bias: float32 [3072], P('col'), may hold values from -3 to 3
- down_weight: float32 [768, 3072], P('row', 'col'), may hold values from -0.109375 to 0.109375
- down_bias: float32 [768], P('col'), may hold values from -3 to 3
- second_gain: float32 [768], P('col'), may hold values from 0.5 to 1.5
- second_shift: float32 [768], P('col'), may hold values from -3 to 3
- cotangent: bfloat16 [32, 768, 1024], P('seqs', 'col', 'row'), may hold values from -6 to 6
Outputs:
- layer_output: bfloat16 [32, 768, 1024], P('seqs', 'col', 'row')
- tokens_grad: bfloat16 [32, 768, 1024], P('seqs', 'col', 'row')
- query_weight_grad: float32 [768, 768], P('row', 'col')
- query_bias_grad: float32 [768], P('col')
- key_weight_grad: float32 [768, 768], P('row', 'col')
- value_weight_grad: float32 [768, 768], P('row', 'col')
- value_bias_grad: float32 [768], P('col')
- out_weight_grad: float32 [768, 768], P('col', 'row')
- out_bias_grad: float32 [768], P('col')
- first_gain_grad: float32 [768], P('col')
- first_shift_grad: float32 [768], P('col')
- up_weight_grad: float32 [768, 3072], P('row', 'col')
- up_bias_grad: float32 [3072], P('col')
- down_weight_grad: float32 [768, 3072], P('row', 'col')
- down_bias_grad: float32 [768], P('col')
- second_gain_grad: float32 [768], P('col')
- second_shift_grad: float32 [768], P('col')
The draws below stay inside these ranges and needn't reach their ends.
Inputs may be any that keep to these rules, and one draw needn't show every extreme that they name: Sequence s holds live tokens in its first lengths[s] slots and padding after; at least one sequence fills all 1024 slots.
All inputs are finite; a program needn't handle non-finite values.
Results may differ from the reference program's by a relative error of at most 0.018.
Values may be sent and summed in bfloat16 or wider, within the bound.
No kernel may reach another device: no remote copies, remote signals or barrier semaphores. Data moves between devices by JAX's collectives and lax.ppermute only.
A program may use at most 384 MiB of HBM per device.

```python
import math
import jax
import jax.numpy as jnp
from jax import lax

D = 768
HEADS = 12
FF = 3072
HD = 64
SLOT = 1024
SEQS = 32


def draw_lengths(key, part):
    key_one, key_two = jax.random.split(jax.random.fold_in(key, 17))
    drawn_lengths = jax.random.randint(key_one, (SEQS,), SLOT // 4, SLOT + 1)
    longest = jax.random.randint(key_two, (), 0, SEQS)
    return jnp.where(jnp.arange(SEQS) == longest, SLOT, drawn_lengths).astype(jnp.int32)


def steps_of(key, extent, cuts, low, top_value):
    level, own = 1.0, jax.random.fold_in(key, 6)
    for axis_at, parts in cuts:
        draws = jnp.exp(jax.random.uniform(jax.random.fold_in(own, axis_at), (parts,), jnp.float32, low / len(cuts), top_value / len(cuts)))
        level = level * jnp.repeat(draws, extent[axis_at] // parts).reshape([-1 if axis == axis_at else 1 for axis in range(len(extent))])
    return level


def gaussian(rng, extent, width, most, shards=(), kind=jnp.bfloat16):
    gain = steps_of(rng, extent, shards, -0.22, 0.18) if shards else 1.0
    entries = jax.random.normal(rng, extent, jnp.float32) * width * gain
    return jnp.minimum(jnp.maximum(entries, -most), most).astype(kind)


def setup_inputs(seed: int = 0) -> dict:
    arg_keys = jax.random.split(jax.random.key(seed), 19)
    tokens = gaussian(arg_keys[0], (SEQS, D, SLOT), 1.0, 6.0, ((0, 4), (1, 4), (2, 2)))
    lengths = draw_lengths(jax.random.fold_in(arg_keys[18], 71), 0)
    query_weight = gaussian(arg_keys[2], (D, D), D ** -0.5, 0.21875, ((0, 2), (1, 4)), jnp.float32)
    query_bias = gaussian(arg_keys[3], (D,), 0.5, 3.0, ((0, 4),), jnp.float32)
    key_weight = gaussian(arg_keys[4], (D, D), D ** -0.5, 0.21875, ((0, 2), (1, 4)), jnp.float32)
    value_weight = gaussian(arg_keys[5], (D, D), D ** -0.5, 0.21875, ((0, 2), (1, 4)), jnp.float32)
    value_bias = gaussian(arg_keys[6], (D,), 0.03, 0.4375, ((0, 4),), jnp.float32)
    out_weight = gaussian(arg_keys[7], (D, D), (max(1, 3 * D // SLOT)) ** -0.5, 4.0, ((0, 4), (1, 2)), jnp.float32)
    out_bias = gaussian(arg_keys[8], (D,), 0.1, 1.5, ((0, 4),), jnp.float32)
    first_gain = jnp.clip(1.0 + 0.1 * jax.random.normal(arg_keys[9], (D,), jnp.float32), 0.5, 1.5)
    first_shift = gaussian(arg_keys[10], (D,), 0.5, 3.0, ((0, 4),), jnp.float32)
    up_weight = gaussian(arg_keys[11], (D, FF), D ** -0.5, 0.21875, ((0, 2), (1, 4)), jnp.float32)
    up_bias = gaussian(arg_keys[12], (FF,), 0.5, 3.0, ((0, 4),), jnp.float32)
    down_weight = gaussian(arg_keys[13], (D, FF), FF ** -0.5, 0.109375, ((0, 2), (1, 4)), jnp.float32)
    down_bias = gaussian(arg_keys[14], (D,), 0.5, 3.0, ((0, 4),), jnp.float32)
    second_gain = jnp.clip(1.0 + 0.1 * jax.random.normal(arg_keys[15], (D,), jnp.float32), 0.5, 1.5)
    second_shift = gaussian(arg_keys[16], (D,), 0.5, 3.0, ((0, 4),), jnp.float32)
    cotangent = gaussian(arg_keys[17], (SEQS, D, SLOT), 1.0, 6.0, ((0, 4), (1, 4), (2, 2)))
    return {"tokens": tokens, "lengths": lengths, "query_weight": query_weight, "query_bias": query_bias, "key_weight": key_weight, "value_weight": value_weight, "value_bias": value_bias, "out_weight": out_weight, "out_bias": out_bias, "first_gain": first_gain, "first_shift": first_shift, "up_weight": up_weight, "up_bias": up_bias, "down_weight": down_weight, "down_bias": down_bias, "second_gain": second_gain, "second_shift": second_shift, "cotangent": cotangent}


epsilon = 1e-05
masked = -1e+30

@jax.custom_vjp
def low(v):
    return lax.optimization_barrier(v.astype(jnp.bfloat16)).astype(jnp.float32)

@jax.custom_vjp
def low_back(v):
    return v

def low_keep(v):
    return (low(v), None)

def low_pass(kept, grad):
    return (grad,)

def back_keep(v):
    return (v, None)

def back_low(kept, grad):
    return (low(grad),)
low.defvjp(low_keep, low_pass)
low_back.defvjp(back_keep, back_low)

def matmul_full(left_side, right_side):
    return jnp.einsum('std,de->ste', left_side, right_side, precision=lax.Precision.HIGHEST)

def layer_norm(hidden, gain_full, shift_full):
    centre = lax.optimization_barrier(jnp.mean(hidden, axis=-1, keepdims=True))
    variance = lax.optimization_barrier(jnp.mean(hidden * hidden, axis=-1, keepdims=True)) - centre * centre
    return (hidden - centre) * lax.rsqrt(variance + epsilon) * gain_full + shift_full

def attend_one(operands):
    query_seq, key_seq, value_seq, allowed_seq = operands
    query_heads = query_seq.reshape(SLOT, HEADS, HD)
    key_heads = key_seq.reshape(SLOT, HEADS, HD)
    value_heads = value_seq.reshape(SLOT, HEADS, HD)
    product = jnp.einsum('qhd,khd->hqk', query_heads, key_heads, precision=lax.Precision.HIGHEST)
    scores = low_back(product * (1.0 / math.sqrt(HD)))
    scores = jnp.where(allowed_seq[None, None, :], scores, masked)
    probs = jax.nn.softmax(scores, axis=-1)
    mixed_heads = jnp.einsum('hqk,khd->qhd', low(probs), value_heads, precision=lax.Precision.HIGHEST)
    return mixed_heads.reshape(SLOT, D)

def layer_forward(token_values, query_weight, query_bias, key_weight, value_weight, value_bias, out_weight, out_bias, first_gain, first_shift, up_weight, up_bias, down_weight, down_bias, second_gain, second_shift, allowed):
    query_all = low(low_back(matmul_full(token_values, low(query_weight)) + query_bias))
    key_all = low(low_back(matmul_full(token_values, low(key_weight))))
    value_all = low(low_back(matmul_full(token_values, low(value_weight)) + value_bias))
    mixed_all = lax.map(jax.checkpoint(attend_one), (query_all, key_all, value_all, allowed))
    mixed_all = low(low_back(mixed_all))
    attn_out = low_back(matmul_full(mixed_all, low(out_weight)) + out_bias)
    first_out = layer_norm(token_values + attn_out, first_gain, first_shift)
    pre_act = low_back(matmul_full(low(first_out), low(up_weight)) + up_bias)
    activated = low(jax.nn.gelu(pre_act, approximate=False))
    branch_out = low_back(matmul_full(activated, low(down_weight).T) + down_bias)
    return layer_norm(first_out + branch_out, second_gain, second_shift)

def reference(tokens, lengths, query_weight, query_bias, key_weight, value_weight, value_bias, out_weight, out_bias, first_gain, first_shift, up_weight, up_bias, down_weight, down_bias, second_gain, second_shift, cotangent):
    positions = jnp.arange(SLOT, dtype=jnp.int32)
    allowed = positions[None, :] < lengths.astype(jnp.int32)[:, None]
    valid = allowed.astype(jnp.float32)[:, :, None]

    def forward(token_values, qw_in, qb_in, kw_in, vw_in, vb_in, ow_in, ob_in, ga_in, sa_in, uw_in, ub_in, dw_in, db_in, gb_in, sb_in):
        return layer_forward(token_values, qw_in, qb_in, kw_in, vw_in, vb_in, ow_in, ob_in, ga_in, sa_in, uw_in, ub_in, dw_in, db_in, gb_in, sb_in, allowed)
    token_major = jnp.transpose(tokens.astype(jnp.float32), (0, 2, 1))
    output, pullback = jax.vjp(forward, token_major, query_weight, query_bias, key_weight, value_weight, value_bias, out_weight, out_bias, first_gain, first_shift, up_weight, up_bias, down_weight, down_bias, second_gain, second_shift)
    grad_major = jnp.transpose(cotangent.astype(jnp.float32), (0, 2, 1))
    grads = pullback(grad_major * valid)
    return (jnp.transpose(output, (0, 2, 1)).astype(jnp.bfloat16), jnp.transpose(grads[0], (0, 2, 1)).astype(jnp.bfloat16), grads[1], grads[2], grads[3], grads[4], grads[5], grads[6], grads[7], grads[8], grads[9], grads[10], grads[11], grads[12], grads[13], grads[14], grads[15])
```

```python
from functools import partial
import math

import jax
import jax.numpy as jnp
from jax import lax
from jax.experimental import pallas as pl
from jax.experimental.pallas import tpu as pltpu
from jax.sharding import PartitionSpec as P

HD = 64
EXTRA = 16

epsilon = 1e-05
masked = -1e30
low = jnp.bfloat16
SCALE = 1.0 / math.sqrt(HD)


def dot_nn(a, b):
    return lax.dot_general(a, b, (((1,), (0,)), ((), ())), preferred_element_type=jnp.float32)


def dot_tn(a, b):
    return lax.dot_general(a, b, (((0,), (0,)), ((), ())), preferred_element_type=jnp.float32)


def dot_nt(a, b):
    return lax.dot_general(a, b, (((1,), (1,)), ((), ())), preferred_element_type=jnp.float32)


def extra_rows(width, rows):
    index = lax.broadcasted_iota(jnp.int32, (EXTRA, width), 0)
    total = jnp.zeros((EXTRA, width), jnp.float32)
    for at, row in enumerate(rows):
        total = jnp.where(index == at, row, total)
    return total.astype(low)


def three_terms(row):
    high = row.astype(low).astype(jnp.float32)
    rest = row - high
    mid = rest.astype(low).astype(jnp.float32)
    return [high, mid, rest - mid]


def key_bias(keys, limit):
    position = lax.broadcasted_iota(jnp.int32, (1, keys), 1)
    return jnp.where(position < limit, 0.0, masked)


def attend_kernel(step, lens, q_ref, k_ref, v_ref, o_ref, lse_ref):
    queries, keys = q_ref.shape[1], k_ref.shape[1]
    one = jnp.ones((1, 1), jnp.float32)
    bias = key_bias(keys, lens[pl.program_id(0)])
    key_side = jnp.concatenate([k_ref[...], extra_rows(keys, [bias])], axis=0)
    value_side = jnp.concatenate([v_ref[...], extra_rows(keys, [one])], axis=0)
    for start in range(0, queries, step):
        part = pl.ds(start, step)
        query_side = jnp.concatenate([q_ref[:, part] * SCALE, extra_rows(step, [one])], axis=0)
        scores = dot_tn(key_side, query_side)
        peak = jnp.max(scores, axis=0, keepdims=True)
        probs = jnp.exp(scores - peak).astype(low)
        mixed = dot_nn(value_side, probs)
        total = mixed[HD : HD + 1]
        o_ref[:, part] = (mixed[:HD] / total).astype(low)
        lse_ref[0, :, part] = peak + jnp.log(total)


def attend_back_kernel(step, lens, q_ref, k_ref, v_ref, o_ref, lse_ref, g_ref, dq_ref, dk_ref, dv_ref, dk_sum, dv_sum):
    queries, keys = q_ref.shape[1], k_ref.shape[1]
    one = jnp.ones((1, 1), jnp.float32)
    bias = key_bias(keys, lens[pl.program_id(0)])
    key_side = jnp.concatenate([k_ref[...], extra_rows(keys, [bias, one, one, one])], axis=0)
    value_side = jnp.concatenate([v_ref[...], extra_rows(keys, [one, one, one])], axis=0)
    for start in range(0, queries, step):
        part = pl.ds(start, step)
        query, grad = q_ref[:, part] * SCALE, g_ref[:, part]
        delta = jnp.sum(
            grad.astype(jnp.float32) * o_ref[:, part].astype(jnp.float32), axis=0, keepdims=True
        )
        query_side = jnp.concatenate(
            [query, extra_rows(step, [one] + three_terms(-lse_ref[0, :, part]))], axis=0
        )
        grad_side = jnp.concatenate([grad, extra_rows(step, three_terms(-delta))], axis=0)
        probs = jnp.exp(dot_tn(key_side, query_side))
        grad_scores = (probs * dot_tn(value_side, grad_side)).astype(low)
        dq_ref[:, part] = (dot_nn(k_ref[...], grad_scores) * SCALE).astype(low)
        dk_part = dot_nt(query, grad_scores)
        dv_part = dot_nt(grad, probs.astype(low))
        if start == 0:
            dk_sum[...] = dk_part
            dv_sum[...] = dv_part
        else:
            dk_sum[...] += dk_part
            dv_sum[...] += dv_part
    dk_ref[...] = dk_sum[...].astype(low)
    dv_ref[...] = dv_sum[...].astype(low)


def query_step(queries, keys):
    for step in (256, 128):
        if queries % step == 0 and step * keys <= 2**20:
            return step
    return queries


def attention(lengths, q, k, v, count):
    rows, tokens = q.shape
    queries, keys = tokens // count, k.shape[1] // count
    heads = rows // HD
    step = query_step(queries, keys)
    spec = lambda size: pl.BlockSpec((HD, size), lambda b, h, lens: (h, b))
    return pl.pallas_call(
        partial(attend_kernel, step),
        grid_spec=pltpu.PrefetchScalarGridSpec(
            num_scalar_prefetch=1,
            grid=(count, heads),
            in_specs=[spec(queries), spec(keys), spec(keys)],
            out_specs=[spec(queries), pl.BlockSpec((1, 1, queries), lambda b, h, lens: (h, 0, b))],
        ),
        out_shape=(
            jax.ShapeDtypeStruct((rows, tokens), low),
            jax.ShapeDtypeStruct((heads, 1, tokens), jnp.float32),
        ),
        cost_estimate=pl.CostEstimate(
            flops=16 * rows * tokens * keys,
            bytes_accessed=8 * rows * tokens,
            transcendentals=heads * tokens * keys,
        ),
        name="attend",
    )(lengths, q, k, v)


def attention_back(lengths, q, k, v, o, lse, grad, count):
    rows, tokens = q.shape
    queries, keys = tokens // count, k.shape[1] // count
    heads = rows // HD
    step = query_step(queries, keys)
    spec = lambda size: pl.BlockSpec((HD, size), lambda b, h, lens: (h, b))
    return pl.pallas_call(
        partial(attend_back_kernel, step),
        grid_spec=pltpu.PrefetchScalarGridSpec(
            num_scalar_prefetch=1,
            grid=(count, heads),
            in_specs=[
                spec(queries),
                spec(keys),
                spec(keys),
                spec(queries),
                pl.BlockSpec((1, 1, queries), lambda b, h, lens: (h, 0, b)),
                spec(queries),
            ],
            out_specs=[spec(queries), spec(keys), spec(keys)],
            scratch_shapes=[pltpu.VMEM((HD, keys), jnp.float32)] * 2,
        ),
        out_shape=(
            jax.ShapeDtypeStruct((rows, tokens), low),
            jax.ShapeDtypeStruct(k.shape, low),
            jax.ShapeDtypeStruct(k.shape, low),
        ),
        cost_estimate=pl.CostEstimate(
            flops=40 * rows * tokens * keys,
            bytes_accessed=16 * rows * tokens,
            transcendentals=heads * tokens * keys,
        ),
        name="attend_back",
    )(lengths, q, k, v, o, lse, grad)


def up_form(weight, rows):
    product = jnp.einsum("cij,it->cjt", weight, rows, preferred_element_type=jnp.float32)
    return product.reshape(-1, rows.shape[1])


def down_form(weight, rows):
    rows = rows.reshape(weight.shape[0], weight.shape[2], rows.shape[1])
    return jnp.einsum("cij,cjt->it", weight, rows, preferred_element_type=jnp.float32)


def normalize(hidden, gain, shift):
    centre = jnp.mean(hidden, axis=0, keepdims=True)
    inverse = lax.rsqrt(jnp.mean(hidden * hidden, axis=0, keepdims=True) - centre * centre + epsilon)
    normed = (hidden - centre) * inverse
    return normed * gain + shift, normed, inverse


def norm_back(grad_out, normed, inverse, gain):
    scaled = grad_out * gain
    return inverse * (
        scaled
        - jnp.mean(scaled, axis=0, keepdims=True)
        - normed * jnp.mean(scaled * normed, axis=0, keepdims=True)
    )


def spread(piece):
    seqs, row, col = (lax.axis_size(name) for name in ("seqs", "row", "col"))
    height = piece.shape[0]
    if height % (16 * seqs) == 0:
        share = height // seqs
        piece = lax.dynamic_slice_in_dim(piece, lax.axis_index("seqs") * share, share, 0)
        whole = lax.all_gather(piece, ("col", "row", "seqs"), axis=0, tiled=True)
    else:
        whole = lax.all_gather(piece, ("col", "row"), axis=0, tiled=True)
    return whole.reshape(col, row * height, piece.shape[1])


def collect(grad):
    seqs = lax.axis_size("seqs")
    grad = lax.psum_scatter(grad.astype(low), "row", scatter_dimension=0, tiled=True)
    if grad.shape[0] % (16 * seqs) == 0:
        grad = lax.psum_scatter(grad, "seqs", scatter_dimension=0, tiled=True)
        grad = lax.psum_scatter(grad, "col", scatter_dimension=1, tiled=True)
        return lax.all_gather(grad, "seqs", axis=0, tiled=True)
    grad = lax.psum_scatter(grad, "col", scatter_dimension=1, tiled=True)
    return lax.psum(grad, "seqs")


def local(
    tokens,
    lengths,
    query_weight,
    query_bias,
    key_weight,
    value_weight,
    value_bias,
    out_weight,
    out_bias,
    first_gain,
    first_shift,
    up_weight,
    up_bias,
    down_weight,
    down_bias,
    second_gain,
    second_shift,
    cotangent,
):
    seq_count, width, rows = tokens.shape
    row, col = lax.axis_size("row"), lax.axis_size("col")
    row_at, col_at = lax.axis_index("row"), lax.axis_index("col")
    members = row * col
    full = width * col
    alone = seq_count % members == 0
    if alone:
        count = seq_count // members
        mine = row * rows
        first = jnp.int32(0)
        own_lengths = lax.dynamic_slice_in_dim(lengths, (col_at * row + row_at) * count, count, 0)
    else:
        count = seq_count // col
        mine = rows
        first = row_at * rows
        own_lengths = lax.dynamic_slice_in_dim(lengths, col_at * count, count, 0)

    def enter(array):
        if alone:
            array = lax.all_to_all(array, ("col", "row"), split_axis=0, concat_axis=0, tiled=True)
            array = array.reshape(col, row, count, width, rows)
            return jnp.transpose(array, (0, 3, 2, 1, 4)).reshape(full, count * mine)
        array = lax.all_to_all(array, "col", split_axis=0, concat_axis=0, tiled=True)
        array = array.reshape(col, count, width, rows)
        return jnp.transpose(array, (0, 2, 1, 3)).reshape(full, count * mine)

    def leave(array):
        if alone:
            array = array.reshape(col, width, count, row, rows)
            array = jnp.transpose(array, (0, 3, 2, 1, 4)).reshape(seq_count, width, rows)
            return lax.all_to_all(array, ("col", "row"), split_axis=0, concat_axis=0, tiled=True)
        array = jnp.transpose(array.reshape(col, width, count, mine), (0, 2, 1, 3))
        array = array.reshape(seq_count, width, rows)
        return lax.all_to_all(array, "col", split_axis=0, concat_axis=0, tiled=True)

    def by_sequence(move, array):
        parts = [move(part) for part in jnp.split(array, count, axis=1)]
        return jnp.concatenate(parts, axis=1)

    def all_keys(array):
        if alone:
            return array
        return by_sequence(lambda part: lax.all_gather(part, "row", axis=1, tiled=True), array)

    def own_keys(array):
        if alone:
            return array
        return by_sequence(
            lambda part: lax.psum_scatter(part, "row", scatter_dimension=1, tiled=True), array
        )

    x_low = enter(tokens)
    qkv_piece = jnp.concatenate([query_weight, key_weight, value_weight], axis=1).astype(low)
    qkv_full = spread(qkv_piece)
    out_full = spread(out_weight.T.astype(low))
    up_full = spread(up_weight.astype(low))
    down_full = spread(down_weight.astype(low))
    small = jnp.concatenate(
        [
            query_bias,
            value_bias,
            out_bias,
            first_gain,
            first_shift,
            down_bias,
            second_gain,
            second_shift,
            up_bias,
        ]
    )
    small = lax.all_gather(small, "col", axis=0, tiled=False)
    vectors = [small[:, at * width : (at + 1) * width].reshape(full, 1) for at in range(8)]
    qb, vb, ob, gain1, shift1, db, gain2, shift2 = vectors
    ub = small[:, 8 * width :].reshape(-1, 1)

    token_count = count * mine
    qkv = up_form(qkv_full, x_low).reshape(col, 3, width, token_count)
    q = (qkv[:, 0].reshape(full, token_count) + qb).astype(low)
    k = qkv[:, 1].reshape(full, token_count).astype(low)
    v = (qkv[:, 2].reshape(full, token_count) + vb).astype(low)
    k_all, v_all = all_keys(k), all_keys(v)
    mixed, lse = attention(own_lengths, q, k_all, v_all, count)
    h1 = x_low.astype(jnp.float32) + (down_form(out_full, mixed) + ob)
    y1, n1, inv1 = normalize(h1, gain1, shift1)
    y1_low = y1.astype(low)
    pre = up_form(up_full, y1_low) + ub
    act, gelu_back = jax.vjp(partial(jax.nn.gelu, approximate=False), pre)
    act_low = act.astype(low)
    h2 = y1 + (down_form(down_full, act_low) + db)
    out, n2, inv2 = normalize(h2, gain2, shift2)
    layer_output = leave(out.astype(low))

    position = first + jnp.arange(mine, dtype=jnp.int32)
    valid = (position[None, :] < own_lengths[:, None]).astype(jnp.float32).reshape(1, token_count)
    g = enter(cotangent).astype(jnp.float32) * valid
    gain2_grad = jnp.sum(g * n2, axis=1)
    shift2_grad = jnp.sum(g, axis=1)
    dh2 = norm_back(g, n2, inv2, gain2)
    dz = dh2.astype(low)
    db_grad = jnp.sum(dz, axis=1, dtype=jnp.float32)
    down_grad = collect(dot_nt(dz, act_low))
    dpre = gelu_back(up_form(down_full, dz))[0].astype(low)
    ub_grad = jnp.sum(dpre, axis=1, dtype=jnp.float32)
    up_grad = collect(dot_nt(y1_low, dpre))
    dy1 = dh2 + down_form(up_full, dpre)
    gain1_grad = jnp.sum(dy1 * n1, axis=1)
    shift1_grad = jnp.sum(dy1, axis=1)
    dh1 = norm_back(dy1, n1, inv1, gain1)
    da = dh1.astype(low)
    ob_grad = jnp.sum(da, axis=1, dtype=jnp.float32)
    out_grad = collect(dot_nt(da, mixed))
    grad_mixed = up_form(out_full, da).astype(low)
    dq, dk, dv = attention_back(own_lengths, q, k_all, v_all, mixed, lse, grad_mixed, count)
    dk, dv = own_keys(dk), own_keys(dv)
    qb_grad = jnp.sum(dq, axis=1, dtype=jnp.float32)
    vb_grad = jnp.sum(dv, axis=1, dtype=jnp.float32)
    block = lambda array: array.reshape(col, width, token_count)
    dqkv = jnp.stack([block(dq), block(dk), block(dv)], axis=1).reshape(3 * full, token_count)
    dx = dh1 + down_form(qkv_full, dqkv)
    tokens_grad = leave(dx.astype(low))
    qkv_grad = collect(dot_nt(x_low, dqkv)).astype(jnp.float32)
    vectors = [qb_grad, vb_grad, ob_grad, gain1_grad, shift1_grad, db_grad, gain2_grad, shift2_grad]
    vectors = [vector.reshape(col, width) for vector in vectors] + [ub_grad.reshape(col, -1)]
    small_grad = lax.psum(jnp.concatenate(vectors, axis=1), ("seqs", "row", "col"))
    small_grad = lax.dynamic_index_in_dim(small_grad, col_at, 0, keepdims=False)
    pieces = [small_grad[at * width : (at + 1) * width] for at in range(8)]
    return (
        layer_output,
        tokens_grad,
        qkv_grad[:, :width],
        pieces[0],
        qkv_grad[:, width : 2 * width],
        qkv_grad[:, 2 * width :],
        pieces[1],
        out_grad.astype(jnp.float32).T,
        pieces[2],
        pieces[3],
        pieces[4],
        up_grad.astype(jnp.float32),
        small_grad[8 * width :],
        down_grad.astype(jnp.float32),
        pieces[5],
        pieces[6],
        pieces[7],
    )


def solution(mesh):
    wide, vector = P("seqs", "col", "row"), P("col")
    square, turned = P("row", "col"), P("col", "row")
    in_specs = (
        wide,
        P("seqs"),
        square,
        vector,
        square,
        square,
        vector,
        turned,
        vector,
        vector,
        vector,
        square,
        vector,
        square,
        vector,
        vector,
        vector,
        wide,
    )
    out_specs = (
        wide,
        wide,
        square,
        vector,
        square,
        square,
        vector,
        turned,
        vector,
        vector,
        vector,
        square,
        vector,
        square,
        vector,
        vector,
        vector,
    )
    return jax.shard_map(local, mesh=mesh, in_specs=in_specs, out_specs=out_specs, check_vma=False)
```

```python
from functools import partial
import math

import jax
import jax.numpy as jnp
from jax import lax
from jax.experimental import pallas as pl
from jax.experimental.pallas import tpu as pltpu
from jax.sharding import PartitionSpec as P

HD = 64
EXTRA = 16
PIECES = 4


epsilon = 1e-05
masked = -1e30
low = jnp.bfloat16
SCALE = 1.0 / math.sqrt(HD)


def dot_nn(a, b):
    return lax.dot_general(a, b, (((1,), (0,)), ((), ())), preferred_element_type=jnp.float32)


def dot_tn(a, b):
    return lax.dot_general(a, b, (((0,), (0,)), ((), ())), preferred_element_type=jnp.float32)


def dot_nt(a, b):
    return lax.dot_general(a, b, (((1,), (1,)), ((), ())), preferred_element_type=jnp.float32)


def extra_rows(width, rows):
    index = lax.broadcasted_iota(jnp.int32, (EXTRA, width), 0)
    total = jnp.zeros((EXTRA, width), jnp.float32)
    for at, row in enumerate(rows):
        total = jnp.where(index == at, row, total)
    return total.astype(low)


def three_terms(row):
    high = row.astype(low).astype(jnp.float32)
    rest = row - high
    mid = rest.astype(low).astype(jnp.float32)
    return [high, mid, rest - mid]


def key_bias(keys, limit):
    position = lax.broadcasted_iota(jnp.int32, (1, keys), 1)
    return jnp.where(position < limit, 0.0, masked)


def attend_kernel(step, lens, q_ref, k_ref, v_ref, o_ref, lse_ref):
    queries, keys = q_ref.shape[1], k_ref.shape[1]
    one = jnp.ones((1, 1), jnp.float32)
    bias = key_bias(keys, lens[pl.program_id(0)])
    key_side = jnp.concatenate([k_ref[...], extra_rows(keys, [bias])], axis=0)
    value_side = jnp.concatenate([v_ref[...], extra_rows(keys, [one])], axis=0)
    for start in range(0, queries, step):
        part = pl.ds(start, step)
        query_side = jnp.concatenate([q_ref[:, part] * SCALE, extra_rows(step, [one])], axis=0)
        scores = dot_tn(key_side, query_side)
        peak = jnp.max(scores, axis=0, keepdims=True)
        probs = jnp.exp(scores - peak).astype(low)
        mixed = dot_nn(value_side, probs)
        total = mixed[HD : HD + 1]
        o_ref[:, part] = (mixed[:HD] / total).astype(low)
        lse_ref[0, :, part] = peak + jnp.log(total)


def attend_back_kernel(step, lens, q_ref, k_ref, v_ref, o_ref, lse_ref, g_ref, dq_ref, dk_ref, dv_ref, dk_sum, dv_sum):
    queries, keys = q_ref.shape[1], k_ref.shape[1]
    one = jnp.ones((1, 1), jnp.float32)
    bias = key_bias(keys, lens[pl.program_id(0)])
    key_side = jnp.concatenate([k_ref[...], extra_rows(keys, [bias, one, one, one])], axis=0)
    value_side = jnp.concatenate([v_ref[...], extra_rows(keys, [one, one, one])], axis=0)
    for start in range(0, queries, step):
        part = pl.ds(start, step)
        query, grad = q_ref[:, part] * SCALE, g_ref[:, part]
        delta = jnp.sum(
            grad.astype(jnp.float32) * o_ref[:, part].astype(jnp.float32), axis=0, keepdims=True
        )
        query_side = jnp.concatenate(
            [query, extra_rows(step, [one] + three_terms(-lse_ref[0, :, part]))], axis=0
        )
        grad_side = jnp.concatenate([grad, extra_rows(step, three_terms(-delta))], axis=0)
        probs = jnp.exp(dot_tn(key_side, query_side))
        grad_scores = (probs * dot_tn(value_side, grad_side)).astype(low)
        dq_ref[:, part] = (dot_nn(k_ref[...], grad_scores) * SCALE).astype(low)
        dk_part = dot_nt(query, grad_scores)
        dv_part = dot_nt(grad, probs.astype(low))
        if start == 0:
            dk_sum[...] = dk_part
            dv_sum[...] = dv_part
        else:
            dk_sum[...] += dk_part
            dv_sum[...] += dv_part
    dk_ref[...] = dk_sum[...].astype(low)
    dv_ref[...] = dv_sum[...].astype(low)


def query_step(queries, keys):
    for step in (256, 128):
        if queries % step == 0 and step * keys <= 2**20:
            return step
    return queries


def attention(lengths, q, k, v, count, pieces=1):
    parts = [attention_part(lengths, q, k, v, count, at, pieces) for at in range(pieces)]
    return tuple(jnp.concatenate(side, axis=0) for side in zip(*parts))


def attention_part(lengths, q, k, v, count, at, pieces):
    rows, tokens = q.shape
    queries, keys = tokens // count, k.shape[1] // count
    rows = rows // pieces
    heads = rows // HD
    begin = at * heads
    step = query_step(queries, keys)
    spec = lambda size: pl.BlockSpec((HD, size), lambda b, h, lens: (h + begin, b))
    out_spec = pl.BlockSpec((HD, queries), lambda b, h, lens: (h, b))
    return pl.pallas_call(
        partial(attend_kernel, step),
        grid_spec=pltpu.PrefetchScalarGridSpec(
            num_scalar_prefetch=1,
            grid=(count, heads),
            in_specs=[spec(queries), spec(keys), spec(keys)],
            out_specs=[out_spec, pl.BlockSpec((1, 1, queries), lambda b, h, lens: (h, 0, b))],
        ),
        out_shape=(
            jax.ShapeDtypeStruct((rows, tokens), low),
            jax.ShapeDtypeStruct((heads, 1, tokens), jnp.float32),
        ),
        cost_estimate=pl.CostEstimate(
            flops=16 * rows * tokens * keys,
            bytes_accessed=8 * rows * tokens,
            transcendentals=heads * tokens * keys,
        ),
        name="attend",
    )(lengths, q, k, v)


def attention_back(lengths, q, k, v, o, lse, grad, count, pieces=1):
    parts = [attention_back_part(lengths, q, k, v, o, lse, grad, count, at, pieces) for at in range(pieces)]
    return tuple(jnp.concatenate(side, axis=0) for side in zip(*parts))


def attention_back_part(lengths, q, k, v, o, lse, grad, count, at, pieces):
    rows, tokens = q.shape
    queries, keys = tokens // count, k.shape[1] // count
    rows = rows // pieces
    heads = rows // HD
    begin = at * heads
    step = query_step(queries, keys)
    spec = lambda size: pl.BlockSpec((HD, size), lambda b, h, lens: (h + begin, b))
    out_spec = lambda size: pl.BlockSpec((HD, size), lambda b, h, lens: (h, b))
    return pl.pallas_call(
        partial(attend_back_kernel, step),
        grid_spec=pltpu.PrefetchScalarGridSpec(
            num_scalar_prefetch=1,
            grid=(count, heads),
            in_specs=[
                spec(queries),
                spec(keys),
                spec(keys),
                spec(queries),
                pl.BlockSpec((1, 1, queries), lambda b, h, lens: (h + begin, 0, b)),
                spec(queries),
            ],
            out_specs=[out_spec(queries), out_spec(keys), out_spec(keys)],
            scratch_shapes=[pltpu.VMEM((HD, keys), jnp.float32)] * 2,
        ),
        out_shape=(
            jax.ShapeDtypeStruct((rows, tokens), low),
            jax.ShapeDtypeStruct((rows, k.shape[1]), low),
            jax.ShapeDtypeStruct((rows, k.shape[1]), low),
        ),
        cost_estimate=pl.CostEstimate(
            flops=40 * rows * tokens * keys,
            bytes_accessed=16 * rows * tokens,
            transcendentals=heads * tokens * keys,
        ),
        name="attend_back",
    )(lengths, q, k, v, o, lse, grad)


def up_form(weight, rows):
    product = jnp.einsum("cij,it->cjt", weight, rows, preferred_element_type=jnp.float32)
    return product.reshape(-1, rows.shape[1])


def down_form(weight, rows):
    rows = rows.reshape(weight.shape[0], weight.shape[2], rows.shape[1])
    return jnp.einsum("cij,cjt->it", weight, rows, preferred_element_type=jnp.float32)


def normalize(hidden, gain, shift):
    centre = jnp.mean(hidden, axis=0, keepdims=True)
    inverse = lax.rsqrt(jnp.mean(hidden * hidden, axis=0, keepdims=True) - centre * centre + epsilon)
    normed = (hidden - centre) * inverse
    return normed * gain + shift, normed, inverse


def norm_back(grad_out, normed, inverse, gain):
    scaled = grad_out * gain
    return inverse * (
        scaled
        - jnp.mean(scaled, axis=0, keepdims=True)
        - normed * jnp.mean(scaled * normed, axis=0, keepdims=True)
    )


def spread(piece):
    seqs, row, col = (lax.axis_size(name) for name in ("seqs", "row", "col"))
    height = piece.shape[0]
    if height % (16 * seqs) == 0:
        share = height // seqs
        piece = lax.dynamic_slice_in_dim(piece, lax.axis_index("seqs") * share, share, 0)
        whole = lax.all_gather(piece, ("col", "row", "seqs"), axis=0, tiled=True)
    else:
        whole = lax.all_gather(piece, ("col", "row"), axis=0, tiled=True)
    return whole.reshape(col, row * height, piece.shape[1])


def collect(grad):
    seqs = lax.axis_size("seqs")
    grad = lax.psum_scatter(grad.astype(low), "row", scatter_dimension=0, tiled=True)
    if grad.shape[0] % (16 * seqs) == 0:
        grad = lax.psum_scatter(grad, "seqs", scatter_dimension=0, tiled=True)
        grad = lax.psum_scatter(grad, "col", scatter_dimension=1, tiled=True)
        return lax.all_gather(grad, "seqs", axis=0, tiled=True)
    grad = lax.psum_scatter(grad, "col", scatter_dimension=1, tiled=True)
    return lax.psum(grad, "seqs")


def swap(array, axis, mask):
    size = lax.axis_size(axis)
    return lax.ppermute(array, axis, [(at, at ^ mask) for at in range(size)])


def shift(array, step):
    size = lax.axis_size("col")
    pairs = [(at, at + step) for at in range(size) if 0 <= at + step < size]
    return lax.ppermute(array, "col", pairs)


def add(*terms):
    return sum(term.astype(jnp.float32) for term in terms).astype(low)


def by_place(blocks):
    own = lax.axis_index("seqs")
    return jnp.stack([lax.dynamic_index_in_dim(blocks, own ^ at, 0, keepdims=False) for at in range(4)])


def fetch_steps(block):
    (block,) = yield [block]
    block = by_place(block)
    col_at = lax.axis_index("col")
    cut = block.shape[1] // 2
    up, down = [block[0]], [block[0]]
    block_row = None
    for _ in range(3):
        flight = [shift(up[-1], 1), shift(down[-1], -1)]
        if block_row is None:
            flight.append(swap(block, "row", 1))
        flight = yield flight
        up.append(flight[0])
        down.append(flight[1])
        if block_row is None:
            block_row = flight[2]
    near = jnp.stack([jnp.where(col_at + at < 4, down[at], up[4 - at]) for at in (1, 2, 3)])
    side, across, near_row = yield [swap(near, "seqs", 1), swap(near, "seqs", 2), swap(near, "row", 1)]
    one, two, side_row, across_row = yield [
        swap(across[:, :cut], "seqs", 1),
        swap(side[:, cut:], "seqs", 2),
        swap(side, "row", 1),
        swap(across, "row", 1),
    ]
    one_row, two_row = yield [swap(one, "row", 1), swap(two, "row", 1)]

    def whole(block, near, side, across, one, two):
        others = jnp.stack([near, side, across, jnp.concatenate([one, two], axis=1)], axis=1)
        return jnp.concatenate([block[None], others], axis=0)

    own = whole(block, near, side, across, one, two)
    other = whole(block_row, near_row, side_row, across_row, one_row, two_row)
    return jnp.concatenate([own, other], axis=3)


def reduce_steps(grad):
    (grad,) = yield [grad]
    n = grad.shape[3] // 2
    (got,) = yield [swap(grad[..., n:], "row", 1)]
    half = add(grad[..., :n], got)
    one, two = half[:2], half[2:]
    got_one, got_two = yield [
        swap(jnp.stack([one[:, 1], one[:, 3]], axis=1), "seqs", 1),
        swap(two[:, 2:], "seqs", 2),
    ]
    one = add(jnp.stack([one[:, 0], one[:, 2]], axis=1), got_one)
    two = add(two[:, :2], got_two)
    got_one, got_two = yield [swap(one[:, 1], "seqs", 2), swap(two[:, 1], "seqs", 1)]
    one, two = add(one[:, 0], got_one), add(two[:, 0], got_two)
    blocks = [one[0], one[1], two[0], two[1]]
    up, down = yield [shift(blocks[3], 1), shift(blocks[1], -1)]
    up, down = yield [shift(add(blocks[2], up), 1), shift(add(blocks[2], down), -1)]
    up, down = yield [shift(add(blocks[1], up), 1), shift(add(blocks[3], down), -1)]
    own = add(blocks[0], up, down)
    cut = own.shape[0] // 2
    side, across = yield [swap(own, "seqs", 1), swap(own, "seqs", 2)]
    one, two = yield [swap(across[:cut], "seqs", 1), swap(side[cut:], "seqs", 2)]
    return by_place(jnp.stack([own, side, across, jnp.concatenate([one, two], axis=0)]))


def sum_steps(array):
    (array,) = yield [array]
    for axis, mask in (("row", 1), ("seqs", 1), ("seqs", 2), ("col", 1), ("col", 2)):
        (got,) = yield [swap(array, axis, mask)]
        array = array + got
    return array


class Chain:
    def __init__(self, steps):
        self.steps, self.result = steps, None
        self.flight = next(steps)

    def advance(self, flight):
        try:
            self.flight = self.steps.send(flight)
        except StopIteration as stop:
            self.flight, self.result = [], stop.value


def stage(main, *chains):
    chains = [chain for chain in chains if chain.result is None]
    main, flights = lax.optimization_barrier((main, [chain.flight for chain in chains]))
    for chain, flight in zip(chains, flights):
        chain.advance(flight)
    return main


def drain(*chains):
    while any(chain.result is None for chain in chains):
        stage(jnp.zeros((), jnp.float32), *chains)


def gelu_both(pre):
    size = jnp.abs(pre)
    bell = jnp.exp(-0.5 * (pre * pre))
    t = 1.0 / (1.0 + (0.3275911 * math.sqrt(0.5)) * size)
    tail = 0.5 * 1.061405429
    for term in (-1.453152027, 1.421413741, -0.284496736, 0.254829592):
        tail = tail * t + 0.5 * term
    tail = tail * t * bell
    phi = jnp.where(pre < 0.0, tail, 1.0 - tail)
    return pre * phi, phi + pre * bell * (1.0 / math.sqrt(2.0 * math.pi))


def local_fast(
    tokens,
    length,
    query_weight,
    query_bias,
    key_weight,
    value_weight,
    value_bias,
    out_weight,
    out_bias,
    first_gain,
    first_shift,
    up_weight,
    up_bias,
    down_weight,
    down_bias,
    second_gain,
    second_shift,
    cotangent,
):
    seq_count, width, slots = tokens.shape
    half = 2 * width
    full, count = 4 * width, 2 * slots
    units = up_weight.shape[1]
    row_at, col_at = lax.axis_index("row"), lax.axis_index("col")

    def turn(array):
        return jnp.where(row_at == 1, jnp.concatenate([array[half:], array[:half]], axis=0), array)

    def enter(array):
        array = lax.all_to_all(array, ("col", "row"), split_axis=0, concat_axis=0, tiled=True)
        array = array.reshape(4, 2, width, slots)
        return turn(jnp.transpose(array, (0, 2, 1, 3)).reshape(full, count))

    def leave(array):
        array = turn(array).reshape(4, width, 2, slots)
        array = jnp.transpose(array, (0, 2, 1, 3)).reshape(seq_count, width, slots)
        return lax.all_to_all(array, ("col", "row"), split_axis=0, concat_axis=0, tiled=True)

    def from_own(array, back=False):
        start = (4 - col_at) % 4 if back else col_at
        return lax.dynamic_slice_in_dim(jnp.concatenate([array, array], axis=0), start, 4, 0)

    def head_order(array, back=False):
        array = from_own(array, back).reshape(4, width // HD, 4, HD // 4, -1)
        return jnp.moveaxis(by_place(jnp.moveaxis(array, 2, 0)), 0, 2).reshape(full, -1)

    def unit_order(array, back=False):
        array = from_own(array, back).reshape(4, 4, units // 4)
        return jnp.moveaxis(by_place(jnp.moveaxis(array, 1, 0)), 0, 1).reshape(4 * units, 1)

    square = [query_weight.T, key_weight.T, value_weight.T, out_weight]
    square = jnp.stack(square).astype(low).reshape(4, width // HD, 4, HD // 4, half)
    square = jnp.transpose(square, (2, 0, 1, 3, 4)).reshape(4, width, half)
    square = Chain(fetch_steps(square))
    up = Chain(fetch_steps(up_weight.T.astype(low).reshape(4, units // 4, half)))
    down = Chain(fetch_steps(down_weight.T.astype(low).reshape(4, units // 4, half)))

    small = [query_bias, value_bias, out_bias, first_gain, first_shift, down_bias, second_gain, second_shift]
    small = jnp.concatenate(small + [up_bias])
    small = jnp.where(lax.broadcasted_iota(jnp.int32, (4, 1), 0) == col_at, small[None], 0.0)
    stage((), square)
    small = small + swap(small, "col", 1)
    stage((), square)
    small = small + swap(small, "col", 2)
    stage((), square)
    tokens = stage(tokens, square)
    vectors = jnp.transpose(small[:, : 8 * width].reshape(4, 8, width), (0, 2, 1))
    bias = head_order(vectors[:, :, :2])
    qb, vb = bias[:, :1], bias[:, 1:]
    vectors = turn(vectors[:, :, 2:].reshape(full, 6))
    ob, gain1, shift1, db, gain2, shift2 = (vectors[:, at : at + 1] for at in range(6))
    ub = unit_order(small[:, 8 * width :])
    x_low = enter(tokens)
    stage((), square)
    stage((), square)
    x_low = stage(x_low, square, up)
    shape = (4, 4, 4, width // HD, HD // 4, full)
    square = jnp.transpose(square.result.reshape(shape), (2, 0, 3, 1, 4, 5)).reshape(4 * full, full)
    qkv_full, out_full = square[: 3 * full], square[3 * full :]

    qkv = dot_nn(qkv_full, x_low)
    q = (qkv[:full] + qb).astype(low)
    k = qkv[full : 2 * full].astype(low)
    v = (qkv[2 * full :] + vb).astype(low)
    parts = []
    for at in range(PIECES):
        if at == 2:
            q, k, v, cotangent = stage((q, k, v, cotangent), *(up, down)[: min(at + 1, 2)])
        else:
            q, k, v = stage((q, k, v), up, down)
        parts.append(attention_part(length, q, k, v, 1, at, PIECES))
        q, parts[-1] = lax.optimization_barrier((q, parts[-1]))
    g = enter(cotangent)
    mixed, lse = (jnp.concatenate(side, axis=0) for side in zip(*parts))
    mixed = stage(mixed, up, down)
    h1 = x_low.astype(jnp.float32) + (dot_tn(out_full, mixed) + ob)
    y1, n1, inv1 = normalize(h1, gain1, shift1)
    y1_low = y1.astype(low)
    y1_low = stage(y1_low, up, down)
    up_full = up.result.reshape(4 * units, full)
    act, slope = gelu_both(dot_nn(up_full, y1_low) + ub)
    act_low, slope = act.astype(low), slope.astype(low)
    act_low = stage(act_low, down)
    drain(down)
    down_full = down.result.reshape(4 * units, full)
    h2 = y1 + (dot_tn(down_full, act_low) + db)
    out, n2, inv2 = normalize(h2, gain2, shift2)
    layer_output = leave(out.astype(low))

    valid = (jnp.arange(count, dtype=jnp.int32)[None, :] < length[:, None]).astype(jnp.float32)
    g = g.astype(jnp.float32) * valid
    gain2_grad = jnp.sum(g * n2, axis=1)
    shift2_grad = jnp.sum(g, axis=1)
    dh2 = norm_back(g, n2, inv2, gain2)
    dz = dh2.astype(low)
    db_grad = jnp.sum(dz, axis=1, dtype=jnp.float32)
    by_share = lambda grad: grad.astype(low).reshape(4, 4, units // 4, full)
    down_grad = Chain(reduce_steps(by_share(dot_nt(act_low, dz))))
    dz = stage(dz, down_grad)
    dpre = (slope.astype(jnp.float32) * dot_nn(down_full, dz)).astype(low)
    ub_grad = jnp.sum(dpre, axis=1, dtype=jnp.float32)
    dpre = stage(dpre, down_grad)
    up_grad = Chain(reduce_steps(by_share(dot_nt(dpre, y1_low))))
    dpre = stage(dpre, up_grad)
    dy1 = dh2 + dot_tn(up_full, dpre)
    gain1_grad = jnp.sum(dy1 * n1, axis=1)
    shift1_grad = jnp.sum(dy1, axis=1)
    dh1 = norm_back(dy1, n1, inv1, gain1)
    da = dh1.astype(low)
    da = stage(da, down_grad, up_grad)
    ob_grad = jnp.sum(da, axis=1, dtype=jnp.float32)
    out_grad = dot_nt(mixed, da).astype(low)
    grad_mixed = dot_nn(out_full, da).astype(low)
    grad_mixed, out_grad = lax.optimization_barrier((grad_mixed, out_grad))
    parts = []
    for at in range(PIECES):
        parts.append(attention_back_part(length, q, k, v, mixed, lse, grad_mixed, 1, at, PIECES))
        grad_mixed, parts[-1] = stage((grad_mixed, parts[-1]), down_grad, up_grad)
    dq, dk, dv = (jnp.concatenate(side, axis=0) for side in zip(*parts))
    dqkv = jnp.concatenate([dq, dk, dv], axis=0)
    square_grad = jnp.concatenate([dot_nt(dqkv, x_low).astype(low), out_grad], axis=0)
    square_grad = square_grad.reshape(4, 4, width // HD, 4, HD // 4, full)
    square_grad = jnp.transpose(square_grad, (1, 3, 0, 2, 4, 5)).reshape(4, 4, width, full)
    square_grad = Chain(reduce_steps(square_grad))
    dqkv = stage(dqkv, square_grad, down_grad, up_grad)
    dx = dh1 + dot_tn(qkv_full, dqkv)
    tokens_grad = leave(dx.astype(low))
    qb_grad = jnp.sum(dq, axis=1, dtype=jnp.float32)
    vb_grad = jnp.sum(dv, axis=1, dtype=jnp.float32)
    bias = head_order(jnp.stack([qb_grad, vb_grad], axis=1).reshape(4, width, 2), True)
    vectors = turn(jnp.stack([ob_grad, gain1_grad, shift1_grad, db_grad, gain2_grad, shift2_grad], axis=1))
    vectors = jnp.concatenate([bias, vectors], axis=1).reshape(4, width, 8)
    vectors = jnp.transpose(vectors, (0, 2, 1)).reshape(4, 8 * width)
    ub_grad = unit_order(ub_grad.reshape(4, units), True).reshape(4, units)
    small_grad = Chain(sum_steps(jnp.concatenate([vectors, ub_grad], axis=1)))
    drain(square_grad, down_grad, up_grad, small_grad)

    small_grad = lax.dynamic_index_in_dim(small_grad.result, col_at, 0, keepdims=False)
    pieces = [small_grad[at * width : (at + 1) * width] for at in range(8)]
    square_grad = square_grad.result.reshape(4, 4, width // HD, HD // 4, half)
    square_grad = jnp.transpose(square_grad, (1, 2, 0, 3, 4)).reshape(4, width, half).astype(jnp.float32)
    block = lambda grad: grad.result.reshape(units, half).astype(jnp.float32).T
    return (
        layer_output,
        tokens_grad,
        square_grad[0].T,
        pieces[0],
        square_grad[1].T,
        square_grad[2].T,
        pieces[1],
        square_grad[3],
        pieces[2],
        pieces[3],
        pieces[4],
        block(up_grad),
        small_grad[8 * width :],
        block(down_grad),
        pieces[5],
        pieces[6],
        pieces[7],
    )


def local(
    tokens,
    lengths,
    query_weight,
    query_bias,
    key_weight,
    value_weight,
    value_bias,
    out_weight,
    out_bias,
    first_gain,
    first_shift,
    up_weight,
    up_bias,
    down_weight,
    down_bias,
    second_gain,
    second_shift,
    cotangent,
):
    seq_count, width, rows = tokens.shape
    row, col = lax.axis_size("row"), lax.axis_size("col")
    row_at, col_at = lax.axis_index("row"), lax.axis_index("col")
    members = row * col
    full = width * col
    alone = seq_count % members == 0
    if alone:
        count = seq_count // members
        mine = row * rows
        first = jnp.int32(0)
        own_lengths = lax.dynamic_slice_in_dim(lengths, (col_at * row + row_at) * count, count, 0)
    else:
        count = seq_count // col
        mine = rows
        first = row_at * rows
        own_lengths = lax.dynamic_slice_in_dim(lengths, col_at * count, count, 0)

    def enter(array):
        if alone:
            array = lax.all_to_all(array, ("col", "row"), split_axis=0, concat_axis=0, tiled=True)
            array = array.reshape(col, row, count, width, rows)
            return jnp.transpose(array, (0, 3, 2, 1, 4)).reshape(full, count * mine)
        array = lax.all_to_all(array, "col", split_axis=0, concat_axis=0, tiled=True)
        array = array.reshape(col, count, width, rows)
        return jnp.transpose(array, (0, 2, 1, 3)).reshape(full, count * mine)

    def leave(array):
        if alone:
            array = array.reshape(col, width, count, row, rows)
            array = jnp.transpose(array, (0, 3, 2, 1, 4)).reshape(seq_count, width, rows)
            return lax.all_to_all(array, ("col", "row"), split_axis=0, concat_axis=0, tiled=True)
        array = jnp.transpose(array.reshape(col, width, count, mine), (0, 2, 1, 3))
        array = array.reshape(seq_count, width, rows)
        return lax.all_to_all(array, "col", split_axis=0, concat_axis=0, tiled=True)

    if alone and lax.axis_size("seqs") == 4 and row == 2 and col == 4 and count == 1 and width == 3 * HD:
        return local_fast(
            tokens,
            own_lengths,
            query_weight,
            query_bias,
            key_weight,
            value_weight,
            value_bias,
            out_weight,
            out_bias,
            first_gain,
            first_shift,
            up_weight,
            up_bias,
            down_weight,
            down_bias,
            second_gain,
            second_shift,
            cotangent,
        )

    def by_sequence(move, array):
        parts = [move(part) for part in jnp.split(array, count, axis=1)]
        return jnp.concatenate(parts, axis=1)

    def all_keys(array):
        if alone:
            return array
        return by_sequence(lambda part: lax.all_gather(part, "row", axis=1, tiled=True), array)

    def own_keys(array):
        if alone:
            return array
        return by_sequence(
            lambda part: lax.psum_scatter(part, "row", scatter_dimension=1, tiled=True), array
        )

    x_low = enter(tokens)
    qkv_piece = jnp.concatenate([query_weight, key_weight, value_weight], axis=1).astype(low)
    qkv_full = spread(qkv_piece)
    out_full = spread(out_weight.T.astype(low))
    up_full = spread(up_weight.astype(low))
    down_full = spread(down_weight.astype(low))
    small = jnp.concatenate(
        [
            query_bias,
            value_bias,
            out_bias,
            first_gain,
            first_shift,
            down_bias,
            second_gain,
            second_shift,
            up_bias,
        ]
    )
    small = lax.all_gather(small, "col", axis=0, tiled=False)
    vectors = [small[:, at * width : (at + 1) * width].reshape(full, 1) for at in range(8)]
    qb, vb, ob, gain1, shift1, db, gain2, shift2 = vectors
    ub = small[:, 8 * width :].reshape(-1, 1)

    token_count = count * mine
    qkv = up_form(qkv_full, x_low).reshape(col, 3, width, token_count)
    q = (qkv[:, 0].reshape(full, token_count) + qb).astype(low)
    k = qkv[:, 1].reshape(full, token_count).astype(low)
    v = (qkv[:, 2].reshape(full, token_count) + vb).astype(low)
    k_all, v_all = all_keys(k), all_keys(v)
    mixed, lse = attention(own_lengths, q, k_all, v_all, count)
    h1 = x_low.astype(jnp.float32) + (down_form(out_full, mixed) + ob)
    y1, n1, inv1 = normalize(h1, gain1, shift1)
    y1_low = y1.astype(low)
    pre = up_form(up_full, y1_low) + ub
    act, gelu_back = jax.vjp(partial(jax.nn.gelu, approximate=False), pre)
    act_low = act.astype(low)
    h2 = y1 + (down_form(down_full, act_low) + db)
    out, n2, inv2 = normalize(h2, gain2, shift2)
    layer_output = leave(out.astype(low))

    position = first + jnp.arange(mine, dtype=jnp.int32)
    valid = (position[None, :] < own_lengths[:, None]).astype(jnp.float32).reshape(1, token_count)
    g = enter(cotangent).astype(jnp.float32) * valid
    gain2_grad = jnp.sum(g * n2, axis=1)
    shift2_grad = jnp.sum(g, axis=1)
    dh2 = norm_back(g, n2, inv2, gain2)
    dz = dh2.astype(low)
    db_grad = jnp.sum(dz, axis=1, dtype=jnp.float32)
    down_grad = collect(dot_nt(dz, act_low))
    dpre = gelu_back(up_form(down_full, dz))[0].astype(low)
    ub_grad = jnp.sum(dpre, axis=1, dtype=jnp.float32)
    up_grad = collect(dot_nt(y1_low, dpre))
    dy1 = dh2 + down_form(up_full, dpre)
    gain1_grad = jnp.sum(dy1 * n1, axis=1)
    shift1_grad = jnp.sum(dy1, axis=1)
    dh1 = norm_back(dy1, n1, inv1, gain1)
    da = dh1.astype(low)
    ob_grad = jnp.sum(da, axis=1, dtype=jnp.float32)
    out_grad = collect(dot_nt(da, mixed))
    grad_mixed = up_form(out_full, da).astype(low)
    dq, dk, dv = attention_back(own_lengths, q, k_all, v_all, mixed, lse, grad_mixed, count)
    dk, dv = own_keys(dk), own_keys(dv)
    qb_grad = jnp.sum(dq, axis=1, dtype=jnp.float32)
    vb_grad = jnp.sum(dv, axis=1, dtype=jnp.float32)
    block = lambda array: array.reshape(col, width, token_count)
    dqkv = jnp.stack([block(dq), block(dk), block(dv)], axis=1).reshape(3 * full, token_count)
    dx = dh1 + down_form(qkv_full, dqkv)
    tokens_grad = leave(dx.astype(low))
    qkv_grad = collect(dot_nt(x_low, dqkv)).astype(jnp.float32)
    vectors = [qb_grad, vb_grad, ob_grad, gain1_grad, shift1_grad, db_grad, gain2_grad, shift2_grad]
    vectors = [vector.reshape(col, width) for vector in vectors] + [ub_grad.reshape(col, -1)]
    small_grad = lax.psum(jnp.concatenate(vectors, axis=1), ("seqs", "row", "col"))
    small_grad = lax.dynamic_index_in_dim(small_grad, col_at, 0, keepdims=False)
    pieces = [small_grad[at * width : (at + 1) * width] for at in range(8)]
    return (
        layer_output,
        tokens_grad,
        qkv_grad[:, :width],
        pieces[0],
        qkv_grad[:, width : 2 * width],
        qkv_grad[:, 2 * width :],
        pieces[1],
        out_grad.astype(jnp.float32).T,
        pieces[2],
        pieces[3],
        pieces[4],
        up_grad.astype(jnp.float32),
        small_grad[8 * width :],
        down_grad.astype(jnp.float32),
        pieces[5],
        pieces[6],
        pieces[7],
    )


def solution(mesh):
    wide, vector = P("seqs", "col", "row"), P("col")
    square, turned = P("row", "col"), P("col", "row")
    in_specs = (
        wide,
        P("seqs"),
        square,
        vector,
        square,
        square,
        vector,
        turned,
        vector,
        vector,
        vector,
        square,
        vector,
        square,
        vector,
        vector,
        vector,
        wide,
    )
    out_specs = (
        wide,
        wide,
        square,
        vector,
        square,
        square,
        vector,
        turned,
        vector,
        vector,
        vector,
        square,
        vector,
        square,
        vector,
        vector,
        vector,
    )
    return jax.shard_map(local, mesh=mesh, in_specs=in_specs, out_specs=out_specs, check_vma=False)
```

```python
from functools import partial
import math

import jax
import jax.numpy as jnp
from jax import lax
from jax.experimental import pallas as pl
from jax.experimental.pallas import tpu as pltpu
from jax.sharding import PartitionSpec as P

HD = 64
EXTRA = 16
PIECES = 4


epsilon = 1e-05
masked = -1e30
low = jnp.bfloat16
SCALE = 1.0 / math.sqrt(HD)


def dot_nn(a, b):
    return lax.dot_general(a, b, (((1,), (0,)), ((), ())), preferred_element_type=jnp.float32)


def dot_tn(a, b):
    return lax.dot_general(a, b, (((0,), (0,)), ((), ())), preferred_element_type=jnp.float32)


def dot_nt(a, b):
    return lax.dot_general(a, b, (((1,), (1,)), ((), ())), preferred_element_type=jnp.float32)


def extra_rows(width, rows):
    index = lax.broadcasted_iota(jnp.int32, (EXTRA, width), 0)
    total = jnp.zeros((EXTRA, width), jnp.float32)
    for at, row in enumerate(rows):
        total = jnp.where(index == at, row, total)
    return total.astype(low)


def three_terms(row):
    high = row.astype(low).astype(jnp.float32)
    rest = row - high
    mid = rest.astype(low).astype(jnp.float32)
    return [high, mid, rest - mid]


def key_bias(keys, limit):
    position = lax.broadcasted_iota(jnp.int32, (1, keys), 1)
    return jnp.where(position < limit, 0.0, masked)


def attend_kernel(step, lens, q_ref, k_ref, v_ref, o_ref, lse_ref):
    queries, keys = q_ref.shape[1], k_ref.shape[1]
    one = jnp.ones((1, 1), jnp.float32)
    bias = key_bias(keys, lens[pl.program_id(0)])
    key_side = jnp.concatenate([k_ref[...], extra_rows(keys, [bias])], axis=0)
    value_side = jnp.concatenate([v_ref[...], extra_rows(keys, [one])], axis=0)
    for start in range(0, queries, step):
        part = pl.ds(start, step)
        query_side = jnp.concatenate([q_ref[:, part] * SCALE, extra_rows(step, [one])], axis=0)
        scores = dot_tn(key_side, query_side)
        peak = jnp.max(scores, axis=0, keepdims=True)
        probs = jnp.exp(scores - peak).astype(low)
        mixed = dot_nn(value_side, probs)
        total = mixed[HD : HD + 1]
        o_ref[:, part] = (mixed[:HD] / total).astype(low)
        lse_ref[0, :, part] = peak + jnp.log(total)


def attend_back_kernel(step, lens, q_ref, k_ref, v_ref, o_ref, lse_ref, g_ref, dq_ref, dk_ref, dv_ref, dk_sum, dv_sum):
    queries, keys = q_ref.shape[1], k_ref.shape[1]
    one = jnp.ones((1, 1), jnp.float32)
    bias = key_bias(keys, lens[pl.program_id(0)])
    key_side = jnp.concatenate([k_ref[...], extra_rows(keys, [bias, one, one, one])], axis=0)
    value_side = jnp.concatenate([v_ref[...], extra_rows(keys, [one, one, one])], axis=0)
    for start in range(0, queries, step):
        part = pl.ds(start, step)
        query, grad = q_ref[:, part] * SCALE, g_ref[:, part]
        delta = jnp.sum(
            grad.astype(jnp.float32) * o_ref[:, part].astype(jnp.float32), axis=0, keepdims=True
        )
        query_side = jnp.concatenate(
            [query, extra_rows(step, [one] + three_terms(-lse_ref[0, :, part]))], axis=0
        )
        grad_side = jnp.concatenate([grad, extra_rows(step, three_terms(-delta))], axis=0)
        probs = jnp.exp(dot_tn(key_side, query_side))
        grad_scores = (probs * dot_tn(value_side, grad_side)).astype(low)
        dq_ref[:, part] = (dot_nn(k_ref[...], grad_scores) * SCALE).astype(low)
        dk_part = dot_nt(query, grad_scores)
        dv_part = dot_nt(grad, probs.astype(low))
        if start == 0:
            dk_sum[...] = dk_part
            dv_sum[...] = dv_part
        else:
            dk_sum[...] += dk_part
            dv_sum[...] += dv_part
    dk_ref[...] = dk_sum[...].astype(low)
    dv_ref[...] = dv_sum[...].astype(low)


def query_step(queries, keys):
    for step in (256, 128):
        if queries % step == 0 and step * keys <= 2**20:
            return step
    return queries


def attention(lengths, q, k, v, count):
    return attention_part(lengths, q, k, v, count, 0, 1)


def attention_part(lengths, q, k, v, count, at, pieces):
    rows, tokens = q.shape
    queries, keys = tokens // count, k.shape[1] // count
    rows = rows // pieces
    heads = rows // HD
    begin = at * heads
    step = query_step(queries, keys)
    spec = lambda size: pl.BlockSpec((HD, size), lambda b, h, lens: (h + begin, b))
    out_spec = pl.BlockSpec((HD, queries), lambda b, h, lens: (h, b))
    return pl.pallas_call(
        partial(attend_kernel, step),
        grid_spec=pltpu.PrefetchScalarGridSpec(
            num_scalar_prefetch=1,
            grid=(count, heads),
            in_specs=[spec(queries), spec(keys), spec(keys)],
            out_specs=[out_spec, pl.BlockSpec((1, 1, queries), lambda b, h, lens: (h, 0, b))],
        ),
        out_shape=(
            jax.ShapeDtypeStruct((rows, tokens), low),
            jax.ShapeDtypeStruct((heads, 1, tokens), jnp.float32),
        ),
        cost_estimate=pl.CostEstimate(
            flops=16 * rows * tokens * keys,
            bytes_accessed=8 * rows * tokens,
            transcendentals=heads * tokens * keys,
        ),
        name="attend",
    )(lengths, q, k, v)


def attention_back(lengths, q, k, v, o, lse, grad, count):
    return attention_back_part(lengths, q, k, v, o, lse, grad, count, 0, 1)


def attention_back_part(lengths, q, k, v, o, lse, grad, count, at, pieces):
    rows, tokens = q.shape
    queries, keys = tokens // count, k.shape[1] // count
    rows = rows // pieces
    heads = rows // HD
    begin = at * heads
    step = query_step(queries, keys)
    spec = lambda size: pl.BlockSpec((HD, size), lambda b, h, lens: (h + begin, b))
    out_spec = lambda size: pl.BlockSpec((HD, size), lambda b, h, lens: (h, b))
    return pl.pallas_call(
        partial(attend_back_kernel, step),
        grid_spec=pltpu.PrefetchScalarGridSpec(
            num_scalar_prefetch=1,
            grid=(count, heads),
            in_specs=[
                spec(queries),
                spec(keys),
                spec(keys),
                spec(queries),
                pl.BlockSpec((1, 1, queries), lambda b, h, lens: (h + begin, 0, b)),
                spec(queries),
            ],
            out_specs=[out_spec(queries), out_spec(keys), out_spec(keys)],
            scratch_shapes=[pltpu.VMEM((HD, keys), jnp.float32)] * 2,
        ),
        out_shape=(
            jax.ShapeDtypeStruct((rows, tokens), low),
            jax.ShapeDtypeStruct((rows, k.shape[1]), low),
            jax.ShapeDtypeStruct((rows, k.shape[1]), low),
        ),
        cost_estimate=pl.CostEstimate(
            flops=40 * rows * tokens * keys,
            bytes_accessed=16 * rows * tokens,
            transcendentals=heads * tokens * keys,
        ),
        name="attend_back",
    )(lengths, q, k, v, o, lse, grad)


def piece_attend(length, qkv, mixed, at):
    full, tokens = qkv.shape[0] // 3, qkv.shape[1]
    heads = full // (4 * HD)
    step = query_step(tokens, tokens)
    base = (at // 2) * 6 * heads + (at % 2) * heads
    spec = lambda kind: pl.BlockSpec((HD, tokens), lambda b, h, lens: (base + 2 * kind * heads + h, 0))
    fresh = mixed is None

    def kernel(lens, q_ref, k_ref, v_ref, *refs):
        o_ref, lse_ref = refs[-2:]
        attend_kernel(step, lens, q_ref, k_ref, v_ref, o_ref, lse_ref)

    return pl.pallas_call(
        kernel,
        grid_spec=pltpu.PrefetchScalarGridSpec(
            num_scalar_prefetch=1,
            grid=(1, heads),
            in_specs=[spec(0), spec(1), spec(2)] + [pl.BlockSpec(memory_space=pl.ANY)] * (not fresh),
            out_specs=[
                pl.BlockSpec((HD, tokens), lambda b, h, lens: (at * heads + h, 0)),
                pl.BlockSpec((1, 1, tokens), lambda b, h, lens: (h, 0, 0)),
            ],
        ),
        out_shape=(
            jax.ShapeDtypeStruct((full, tokens), low),
            jax.ShapeDtypeStruct((heads, 1, tokens), jnp.float32),
        ),
        input_output_aliases={} if fresh else {4: 0},
        cost_estimate=pl.CostEstimate(
            flops=4 * full * tokens * tokens,
            bytes_accessed=2 * full * tokens,
            transcendentals=heads * tokens * tokens,
        ),
        name="attend",
    )(*((length, qkv, qkv, qkv) + (() if fresh else (mixed,))))


def piece_attend_back(length, qkv, mixed, lse, grad, dqkv, at):
    full, tokens = qkv.shape[0] // 3, qkv.shape[1]
    heads = full // (4 * HD)
    step = query_step(tokens, tokens)
    base = (at // 2) * 6 * heads + (at % 2) * heads
    spec = lambda kind: pl.BlockSpec((HD, tokens), lambda b, h, lens: (base + 2 * kind * heads + h, 0))
    mine = pl.BlockSpec((HD, tokens), lambda b, h, lens: (at * heads + h, 0))
    fresh = dqkv is None

    def kernel(lens, q_ref, k_ref, v_ref, o_ref, lse_ref, g_ref, *refs):
        d_ref, dk_sum, dv_sum = refs[-3:]
        attend_back_kernel(
            step,
            lens,
            q_ref,
            k_ref,
            v_ref,
            o_ref,
            lse_ref,
            g_ref,
            d_ref.at[0],
            d_ref.at[1],
            d_ref.at[2],
            dk_sum,
            dv_sum,
        )

    return pl.pallas_call(
        kernel,
        grid_spec=pltpu.PrefetchScalarGridSpec(
            num_scalar_prefetch=1,
            grid=(1, heads),
            in_specs=[
                spec(0),
                spec(1),
                spec(2),
                mine,
                pl.BlockSpec((1, 1, tokens), lambda b, h, lens: (h, 0, 0)),
                mine,
            ]
            + [pl.BlockSpec(memory_space=pl.ANY)] * (not fresh),
            out_specs=pl.BlockSpec((3, HD, tokens), lambda b, h, lens: (0, (at % 2) * heads + h, 0)),
            scratch_shapes=[pltpu.VMEM((HD, tokens), jnp.float32)] * 2,
        ),
        out_shape=jax.ShapeDtypeStruct((3, full // 2, tokens), low),
        input_output_aliases={} if fresh else {7: 0},
        cost_estimate=pl.CostEstimate(
            flops=10 * full * tokens * tokens,
            bytes_accessed=4 * full * tokens,
            transcendentals=heads * tokens * tokens,
        ),
        name="attend_back",
    )(*((length, qkv, qkv, qkv, mixed, lse, grad) + (() if fresh else (dqkv,))))


def up_form(weight, rows):
    product = jnp.einsum("cij,it->cjt", weight, rows, preferred_element_type=jnp.float32)
    return product.reshape(-1, rows.shape[1])


def down_form(weight, rows):
    rows = rows.reshape(weight.shape[0], weight.shape[2], rows.shape[1])
    return jnp.einsum("cij,cjt->it", weight, rows, preferred_element_type=jnp.float32)


def normalize(hidden, gain, shift):
    centre = jnp.mean(hidden, axis=0, keepdims=True)
    inverse = lax.rsqrt(jnp.mean(hidden * hidden, axis=0, keepdims=True) - centre * centre + epsilon)
    normed = (hidden - centre) * inverse
    return normed * gain + shift, normed, inverse


def norm_back(grad_out, normed, inverse, gain):
    scaled = grad_out * gain
    return inverse * (
        scaled
        - jnp.mean(scaled, axis=0, keepdims=True)
        - normed * jnp.mean(scaled * normed, axis=0, keepdims=True)
    )


def spread(piece):
    seqs, row, col = (lax.axis_size(name) for name in ("seqs", "row", "col"))
    height = piece.shape[0]
    if height % (16 * seqs) == 0:
        share = height // seqs
        piece = lax.dynamic_slice_in_dim(piece, lax.axis_index("seqs") * share, share, 0)
        whole = lax.all_gather(piece, ("col", "row", "seqs"), axis=0, tiled=True)
    else:
        whole = lax.all_gather(piece, ("col", "row"), axis=0, tiled=True)
    return whole.reshape(col, row * height, piece.shape[1])


def collect(grad):
    seqs = lax.axis_size("seqs")
    grad = lax.psum_scatter(grad.astype(low), "row", scatter_dimension=0, tiled=True)
    if grad.shape[0] % (16 * seqs) == 0:
        grad = lax.psum_scatter(grad, "seqs", scatter_dimension=0, tiled=True)
        grad = lax.psum_scatter(grad, "col", scatter_dimension=1, tiled=True)
        return lax.all_gather(grad, "seqs", axis=0, tiled=True)
    grad = lax.psum_scatter(grad, "col", scatter_dimension=1, tiled=True)
    return lax.psum(grad, "seqs")


def swap(array, axis, mask):
    size = lax.axis_size(axis)
    return lax.ppermute(array, axis, [(at, at ^ mask) for at in range(size)])


def add(*terms):
    return sum(term.astype(jnp.float32) for term in terms).astype(low)


def by_place(blocks, axis):
    own = lax.axis_index(axis)
    return jnp.stack([lax.dynamic_index_in_dim(blocks, own ^ at, 0, keepdims=False) for at in range(4)])


def fetch_steps(block):
    (block,) = yield [block]
    own = lax.dynamic_index_in_dim(block, lax.axis_index("seqs"), 0, keepdims=True)
    cut = own.shape[1] // 2
    (got,) = yield [swap(own, "col", 1)]
    own = jnp.concatenate([own, got], axis=0)
    (got,) = yield [swap(own, "col", 2)]
    own = jnp.concatenate([own, got], axis=0)
    side, across = yield [swap(own, "seqs", 1), swap(own, "seqs", 2)]
    one, two = yield [swap(across[:, :cut], "seqs", 1), swap(side[:, cut:], "seqs", 2)]
    own = jnp.stack([own, side, across, jnp.concatenate([one, two], axis=1)], axis=1)
    (other,) = yield [swap(own, "row", 1)]
    return jnp.concatenate([own, other], axis=3)


def plane_steps(keep, send):
    keep, send = yield [keep, send]
    (got,) = yield [swap(send, "row", 1)]
    keep = add(keep, got)
    half = keep.shape[0] // 2
    one, two = keep[:half], keep[half:]
    got_one, got_two = yield [
        swap(jnp.stack([one[:, 1], one[:, 3]], axis=1), "seqs", 1),
        swap(two[:, 2:], "seqs", 2),
    ]
    one_far, two_far = add(one[:, 2], got_one[:, 1]), add(two[:, 1], got_two[:, 1])
    one, two = add(one[:, 0], got_one[:, 0]), add(two[:, 0], got_two[:, 0])
    got_one, got_two = yield [swap(one_far, "seqs", 2), swap(two_far, "seqs", 1)]
    return jnp.concatenate([add(one, got_one), add(two, got_two)], axis=0)


def far_steps(keep, send):
    blocks = yield from plane_steps(keep, send)
    (got,) = yield [swap(blocks, "col", 2)]
    return got


def end_steps(own, far):
    near, (got,) = own[0], (yield [swap(add(own[1], far[1]), "col", 1)])
    near = add(near, far[0], got)
    cut = near.shape[0] // 2
    side, across = yield [swap(near, "seqs", 1), swap(near, "seqs", 2)]
    one, two = yield [swap(across[:cut], "seqs", 1), swap(side[cut:], "seqs", 2)]
    return by_place(jnp.stack([near, side, across, jnp.concatenate([one, two], axis=0)]), "seqs")


def reduce_steps(keep, send):
    blocks = yield from plane_steps(keep, send)
    (far,) = yield [swap(blocks[2:], "col", 2)]
    return (yield from end_steps(blocks[:2], far))


def near_steps(keep, send, far):
    own = yield from plane_steps(keep, send)
    return (yield from end_steps(own, far.result))


def sum_steps(array):
    (array,) = yield [array]
    for axis, mask in (("row", 1), ("seqs", 1), ("seqs", 2), ("col", 1), ("col", 2)):
        (got,) = yield [swap(array, axis, mask)]
        array = array + got
    return array


class Chain:
    def __init__(self, steps):
        self.steps, self.result = steps, None
        self.flight = next(steps)

    def advance(self, flight):
        try:
            self.flight = self.steps.send(flight)
        except StopIteration as stop:
            self.flight, self.result = [], stop.value


def stage(main, *chains):
    chains = [chain for chain in chains if chain.result is None]
    main, flights = lax.optimization_barrier((main, [chain.flight for chain in chains]))
    for chain, flight in zip(chains, flights):
        chain.advance(flight)
    return main


def drain(*chains):
    while any(chain.result is None for chain in chains):
        stage(jnp.zeros((), jnp.float32), *chains)


def gelu_both(pre):
    size = jnp.abs(pre)
    bell = jnp.exp(-0.5 * (pre * pre))
    t = 1.0 / (1.0 + (0.3275911 * math.sqrt(0.5)) * size)
    tail = 0.5 * 1.061405429
    for term in (-1.453152027, 1.421413741, -0.284496736, 0.254829592):
        tail = tail * t + 0.5 * term
    tail = tail * t * bell
    phi = jnp.where(pre < 0.0, tail, 1.0 - tail)
    return pre * phi, phi + pre * bell * (1.0 / math.sqrt(2.0 * math.pi))


def local_fast(
    tokens,
    length,
    query_weight,
    query_bias,
    key_weight,
    value_weight,
    value_bias,
    out_weight,
    out_bias,
    first_gain,
    first_shift,
    up_weight,
    up_bias,
    down_weight,
    down_bias,
    second_gain,
    second_shift,
    cotangent,
):
    seq_count, width, slots = tokens.shape
    half = 2 * width
    full, count = 4 * width, 2 * slots
    units = up_weight.shape[1]
    row_at, col_at = lax.axis_index("row"), lax.axis_index("col")

    def turn(array):
        return jnp.where(row_at == 1, jnp.concatenate([array[half:], array[:half]], axis=0), array)

    def enter(array):
        array = lax.all_to_all(array, ("col", "row"), split_axis=0, concat_axis=0, tiled=True)
        array = array.reshape(4, 2, width, slots)
        array = jnp.concatenate([array[:, 0], array[:, 1]], axis=2)
        return turn(array.reshape(full, count))

    def leave(array):
        array = turn(array).reshape(4, width, count)
        array = jnp.stack([array[:, :, :slots], array[:, :, slots:]], axis=1)
        array = array.reshape(seq_count, width, slots)
        return lax.all_to_all(array, ("col", "row"), split_axis=0, concat_axis=0, tiled=True)

    def head_order(array):
        array = by_place(array, "col").reshape(4, width // HD, 4, HD // 4, -1)
        return jnp.moveaxis(by_place(jnp.moveaxis(array, 2, 0), "seqs"), 0, 2).reshape(full, -1)

    def unit_order(array):
        array = by_place(array, "col").reshape(4, 4, units // 4)
        return jnp.moveaxis(by_place(jnp.moveaxis(array, 1, 0), "seqs"), 0, 1).reshape(4 * units, 1)

    heads = width // HD
    square = [query_weight.T, key_weight.T, value_weight.T, out_weight]
    square = jnp.stack(square).astype(low).reshape(4, heads, 4, HD // 4, half)
    square = jnp.transpose(square, (2, 0, 1, 3, 4)).reshape(4, width, half)
    square = Chain(fetch_steps(square))
    up = Chain(fetch_steps(up_weight.T.astype(low).reshape(4, units // 4, half)))
    down = Chain(fetch_steps(down_weight.T.astype(low).reshape(4, units // 4, half)))

    small = [query_bias, value_bias, out_bias, first_gain, first_shift, down_bias, second_gain, second_shift]
    small = jnp.concatenate(small + [up_bias])
    small = jnp.where(lax.broadcasted_iota(jnp.int32, (4, 1), 0) == col_at, small[None], 0.0)
    small = stage(small, square)
    got = swap(small, "col", 1)
    got = stage(got, square)
    small = small + got
    got = swap(small, "col", 2)
    tokens, got = stage((tokens, got), square)
    small = small + got
    x_low = enter(tokens)
    vectors = jnp.transpose(small[:, : 8 * width].reshape(4, 8, width), (0, 2, 1))
    bias = head_order(vectors[:, :, :2]).reshape(2, 2 * width, 2)
    bias = jnp.stack([bias[:, :, 0], jnp.zeros_like(bias[:, :, 0]), bias[:, :, 1]], axis=1).reshape(3 * full, 1)
    vectors = turn(vectors[:, :, 2:].reshape(full, 6))
    ob, gain1, shift1, db, gain2, shift2 = (vectors[:, at : at + 1] for at in range(6))
    ub = unit_order(small[:, 8 * width :])
    stage((), square)
    stage((), square)
    x_low = stage(x_low, square, up)
    square = square.result.reshape(2, 2, 4, 4, heads, HD // 4, full)
    qkv_full = jnp.transpose(square[:, :, :, :3], (0, 3, 1, 4, 2, 5, 6)).reshape(3 * full, full)
    out_full = jnp.transpose(square[:, :, :, 3], (0, 1, 3, 2, 4, 5)).reshape(full, full)

    qkv = (dot_nn(qkv_full, x_low) + bias).astype(low)
    mixed, lse = None, []
    for at in range(PIECES):
        chains = (up,) if at == 0 else (up, down)
        if at == 3:
            qkv, mixed, cotangent = stage((qkv, mixed, cotangent), *chains)
        else:
            qkv, mixed = stage((qkv, mixed), *chains)
        mixed, part = piece_attend(length, qkv, mixed, at)
        lse.append(part)
    g = lax.optimization_barrier(enter(cotangent))
    mixed = stage(mixed, up, down)
    h1 = x_low.astype(jnp.float32) + (dot_tn(out_full, mixed) + ob)
    y1, n1, inv1 = normalize(h1, gain1, shift1)
    y1_low = stage(y1.astype(low), down)
    up_full = up.result.reshape(4 * units, full)
    act, slope = gelu_both(dot_nn(up_full, y1_low) + ub)
    act_low, slope = stage((act.astype(low), slope.astype(low)), down)
    down_full = down.result.reshape(4 * units, full)
    h2 = y1 + (dot_tn(down_full, act_low) + db)
    out, n2, inv2 = normalize(h2, gain2, shift2)
    layer_output = leave(out.astype(low))

    ones = jnp.ones((count, 128), low)
    token_sum = lambda array: dot_nn(array, ones)[:, 0]
    valid = (jnp.arange(count, dtype=jnp.int32)[None, :] < length[:, None]).astype(jnp.float32)
    g = g.astype(jnp.float32) * valid
    gain2_grad = jnp.sum(g * n2, axis=1)
    shift2_grad = jnp.sum(g, axis=1)
    dh2 = norm_back(g, n2, inv2, gain2)
    dz = dh2.astype(low)
    db_grad = token_sum(dz)
    by_share = lambda grad: grad.astype(low).reshape(4, 4, units // 4, half)

    def halves(one, two):
        return by_share(dot_nt(one, two[:half])), by_share(dot_nt(one, two[half:]))

    down_grad = Chain(reduce_steps(*halves(act_low, dz)))
    dz = stage(dz, down_grad)
    dpre = (slope.astype(jnp.float32) * dot_nn(down_full, dz)).astype(low)
    dpre = stage(dpre, down_grad)
    ub_grad = token_sum(dpre)
    up_grad = Chain(reduce_steps(*halves(dpre, y1_low)))
    dpre = stage(dpre, up_grad)
    dy1 = dh2 + dot_tn(up_full, dpre)
    gain1_grad = jnp.sum(dy1 * n1, axis=1)
    shift1_grad = jnp.sum(dy1, axis=1)
    dh1 = norm_back(dy1, n1, inv1, gain1)
    da = dh1.astype(low)
    da = stage(da, down_grad, up_grad)
    ob_grad = token_sum(da)
    out_grad = [dot_nt(mixed, part).astype(low) for part in (da[:half], da[half:])]
    grad_mixed = dot_nn(out_full, da).astype(low)
    grad_mixed, out_grad = stage((grad_mixed, out_grad), down_grad)

    def square_share(pair, dqkv):
        rows = dqkv.reshape(6 * width, count)
        shares = []
        for part, other in zip((x_low[:half], x_low[half:]), out_grad):
            grad = dot_nt(rows, part).astype(low).reshape(3, 2 * width, half)
            other = other[2 * width * pair : 2 * width * (pair + 1)]
            grad = jnp.concatenate([grad, other[None]], axis=0).reshape(4, 2, heads, 4, HD // 4, half)
            shares.append(jnp.transpose(grad, (1, 3, 0, 2, 4, 5)).reshape(2, 4, width, half))
        return shares

    dqkv = piece_attend_back(length, qkv, mixed, lse[2], grad_mixed, None, 2)
    grad_mixed, dqkv = stage((grad_mixed, dqkv), down_grad, up_grad)
    dqkv = piece_attend_back(length, qkv, mixed, lse[3], grad_mixed, dqkv, 3)
    grad_mixed, dqkv, layer_output = stage((grad_mixed, dqkv, layer_output), down_grad, up_grad)
    far = Chain(far_steps(*square_share(1, dqkv)))
    dx = dh1 + dot_tn(qkv_full[6 * width :], dqkv.reshape(6 * width, count))
    v_sums = [token_sum(dqkv[2])]
    q_sums = [token_sum(dqkv[0])]
    grad_mixed, dx = stage((grad_mixed, dx), far, down_grad)
    dqkv = piece_attend_back(length, qkv, mixed, lse[0], grad_mixed, None, 0)
    grad_mixed, dqkv = stage((grad_mixed, dqkv), far, down_grad, up_grad)
    dqkv = piece_attend_back(length, qkv, mixed, lse[1], grad_mixed, dqkv, 1)
    dqkv = stage(dqkv, far, down_grad, up_grad)
    square_grad = Chain(near_steps(*square_share(0, dqkv), far))
    dqkv, dx = stage((dqkv, dx), square_grad, up_grad)
    dx = dx + dot_tn(qkv_full[: 6 * width], dqkv.reshape(6 * width, count))
    tokens_grad = leave(dx.astype(low))
    v_sums = jnp.concatenate([token_sum(dqkv[2])] + v_sums)
    q_sums = jnp.concatenate([token_sum(dqkv[0])] + q_sums)
    bias = head_order(jnp.stack([q_sums, v_sums], axis=1).reshape(4, width, 2))
    vectors = turn(jnp.stack([ob_grad, gain1_grad, shift1_grad, db_grad, gain2_grad, shift2_grad], axis=1))
    vectors = jnp.concatenate([bias, vectors], axis=1).reshape(4, width, 8)
    vectors = jnp.transpose(vectors, (0, 2, 1)).reshape(4, 8 * width)
    ub_grad = unit_order(ub_grad.reshape(4, units)).reshape(4, units)
    small_grad = Chain(sum_steps(jnp.concatenate([vectors, ub_grad], axis=1)))
    drain(square_grad, far, down_grad, up_grad, small_grad)

    small_grad = lax.dynamic_index_in_dim(small_grad.result, col_at, 0, keepdims=False)
    pieces = [small_grad[at * width : (at + 1) * width] for at in range(8)]
    square_grad = square_grad.result.reshape(4, 4, heads, HD // 4, half)
    square_grad = jnp.transpose(square_grad, (1, 2, 0, 3, 4)).reshape(4, width, half).astype(jnp.float32)
    block = lambda grad: grad.result.reshape(units, half).astype(jnp.float32).T
    return (
        layer_output,
        tokens_grad,
        square_grad[0].T,
        pieces[0],
        square_grad[1].T,
        square_grad[2].T,
        pieces[1],
        square_grad[3],
        pieces[2],
        pieces[3],
        pieces[4],
        block(up_grad),
        small_grad[8 * width :],
        block(down_grad),
        pieces[5],
        pieces[6],
        pieces[7],
    )


def local(
    tokens,
    lengths,
    query_weight,
    query_bias,
    key_weight,
    value_weight,
    value_bias,
    out_weight,
    out_bias,
    first_gain,
    first_shift,
    up_weight,
    up_bias,
    down_weight,
    down_bias,
    second_gain,
    second_shift,
    cotangent,
):
    seq_count, width, rows = tokens.shape
    row, col = lax.axis_size("row"), lax.axis_size("col")
    row_at, col_at = lax.axis_index("row"), lax.axis_index("col")
    members = row * col
    full = width * col
    alone = seq_count % members == 0
    if alone:
        count = seq_count // members
        mine = row * rows
        first = jnp.int32(0)
        own_lengths = lax.dynamic_slice_in_dim(lengths, (col_at * row + row_at) * count, count, 0)
    else:
        count = seq_count // col
        mine = rows
        first = row_at * rows
        own_lengths = lax.dynamic_slice_in_dim(lengths, col_at * count, count, 0)

    def enter(array):
        if alone:
            array = lax.all_to_all(array, ("col", "row"), split_axis=0, concat_axis=0, tiled=True)
            array = array.reshape(col, row, count, width, rows)
            return jnp.transpose(array, (0, 3, 2, 1, 4)).reshape(full, count * mine)
        array = lax.all_to_all(array, "col", split_axis=0, concat_axis=0, tiled=True)
        array = array.reshape(col, count, width, rows)
        return jnp.transpose(array, (0, 2, 1, 3)).reshape(full, count * mine)

    def leave(array):
        if alone:
            array = array.reshape(col, width, count, row, rows)
            array = jnp.transpose(array, (0, 3, 2, 1, 4)).reshape(seq_count, width, rows)
            return lax.all_to_all(array, ("col", "row"), split_axis=0, concat_axis=0, tiled=True)
        array = jnp.transpose(array.reshape(col, width, count, mine), (0, 2, 1, 3))
        array = array.reshape(seq_count, width, rows)
        return lax.all_to_all(array, "col", split_axis=0, concat_axis=0, tiled=True)

    if alone and lax.axis_size("seqs") == 4 and row == 2 and col == 4 and count == 1 and width == 3 * HD:
        return local_fast(
            tokens,
            own_lengths,
            query_weight,
            query_bias,
            key_weight,
            value_weight,
            value_bias,
            out_weight,
            out_bias,
            first_gain,
            first_shift,
            up_weight,
            up_bias,
            down_weight,
            down_bias,
            second_gain,
            second_shift,
            cotangent,
        )

    def by_sequence(move, array):
        parts = [move(part) for part in jnp.split(array, count, axis=1)]
        return jnp.concatenate(parts, axis=1)

    def all_keys(array):
        if alone:
            return array
        return by_sequence(lambda part: lax.all_gather(part, "row", axis=1, tiled=True), array)

    def own_keys(array):
        if alone:
            return array
        return by_sequence(
            lambda part: lax.psum_scatter(part, "row", scatter_dimension=1, tiled=True), array
        )

    x_low = enter(tokens)
    qkv_piece = jnp.concatenate([query_weight, key_weight, value_weight], axis=1).astype(low)
    qkv_full = spread(qkv_piece)
    out_full = spread(out_weight.T.astype(low))
    up_full = spread(up_weight.astype(low))
    down_full = spread(down_weight.astype(low))
    small = jnp.concatenate(
        [
            query_bias,
            value_bias,
            out_bias,
            first_gain,
            first_shift,
            down_bias,
            second_gain,
            second_shift,
            up_bias,
        ]
    )
    small = lax.all_gather(small, "col", axis=0, tiled=False)
    vectors = [small[:, at * width : (at + 1) * width].reshape(full, 1) for at in range(8)]
    qb, vb, ob, gain1, shift1, db, gain2, shift2 = vectors
    ub = small[:, 8 * width :].reshape(-1, 1)

    token_count = count * mine
    qkv = up_form(qkv_full, x_low).reshape(col, 3, width, token_count)
    q = (qkv[:, 0].reshape(full, token_count) + qb).astype(low)
    k = qkv[:, 1].reshape(full, token_count).astype(low)
    v = (qkv[:, 2].reshape(full, token_count) + vb).astype(low)
    k_all, v_all = all_keys(k), all_keys(v)
    mixed, lse = attention(own_lengths, q, k_all, v_all, count)
    h1 = x_low.astype(jnp.float32) + (down_form(out_full, mixed) + ob)
    y1, n1, inv1 = normalize(h1, gain1, shift1)
    y1_low = y1.astype(low)
    pre = up_form(up_full, y1_low) + ub
    act, gelu_back = jax.vjp(partial(jax.nn.gelu, approximate=False), pre)
    act_low = act.astype(low)
    h2 = y1 + (down_form(down_full, act_low) + db)
    out, n2, inv2 = normalize(h2, gain2, shift2)
    layer_output = leave(out.astype(low))

    position = first + jnp.arange(mine, dtype=jnp.int32)
    valid = (position[None, :] < own_lengths[:, None]).astype(jnp.float32).reshape(1, token_count)
    g = enter(cotangent).astype(jnp.float32) * valid
    gain2_grad = jnp.sum(g * n2, axis=1)
    shift2_grad = jnp.sum(g, axis=1)
    dh2 = norm_back(g, n2, inv2, gain2)
    dz = dh2.astype(low)
    db_grad = jnp.sum(dz, axis=1, dtype=jnp.float32)
    down_grad = collect(dot_nt(dz, act_low))
    dpre = gelu_back(up_form(down_full, dz))[0].astype(low)
    ub_grad = jnp.sum(dpre, axis=1, dtype=jnp.float32)
    up_grad = collect(dot_nt(y1_low, dpre))
    dy1 = dh2 + down_form(up_full, dpre)
    gain1_grad = jnp.sum(dy1 * n1, axis=1)
    shift1_grad = jnp.sum(dy1, axis=1)
    dh1 = norm_back(dy1, n1, inv1, gain1)
    da = dh1.astype(low)
    ob_grad = jnp.sum(da, axis=1, dtype=jnp.float32)
    out_grad = collect(dot_nt(da, mixed))
    grad_mixed = up_form(out_full, da).astype(low)
    dq, dk, dv = attention_back(own_lengths, q, k_all, v_all, mixed, lse, grad_mixed, count)
    dk, dv = own_keys(dk), own_keys(dv)
    qb_grad = jnp.sum(dq, axis=1, dtype=jnp.float32)
    vb_grad = jnp.sum(dv, axis=1, dtype=jnp.float32)
    block = lambda array: array.reshape(col, width, token_count)
    dqkv = jnp.stack([block(dq), block(dk), block(dv)], axis=1).reshape(3 * full, token_count)
    dx = dh1 + down_form(qkv_full, dqkv)
    tokens_grad = leave(dx.astype(low))
    qkv_grad = collect(dot_nt(x_low, dqkv)).astype(jnp.float32)
    vectors = [qb_grad, vb_grad, ob_grad, gain1_grad, shift1_grad, db_grad, gain2_grad, shift2_grad]
    vectors = [vector.reshape(col, width) for vector in vectors] + [ub_grad.reshape(col, -1)]
    small_grad = lax.psum(jnp.concatenate(vectors, axis=1), ("seqs", "row", "col"))
    small_grad = lax.dynamic_index_in_dim(small_grad, col_at, 0, keepdims=False)
    pieces = [small_grad[at * width : (at + 1) * width] for at in range(8)]
    return (
        layer_output,
        tokens_grad,
        qkv_grad[:, :width],
        pieces[0],
        qkv_grad[:, width : 2 * width],
        qkv_grad[:, 2 * width :],
        pieces[1],
        out_grad.astype(jnp.float32).T,
        pieces[2],
        pieces[3],
        pieces[4],
        up_grad.astype(jnp.float32),
        small_grad[8 * width :],
        down_grad.astype(jnp.float32),
        pieces[5],
        pieces[6],
        pieces[7],
    )


def solution(mesh):
    wide, vector = P("seqs", "col", "row"), P("col")
    square, turned = P("row", "col"), P("col", "row")
    in_specs = (
        wide,
        P("seqs"),
        square,
        vector,
        square,
        square,
        vector,
        turned,
        vector,
        vector,
        vector,
        square,
        vector,
        square,
        vector,
        vector,
        vector,
        wide,
    )
    out_specs = (
        wide,
        wide,
        square,
        vector,
        square,
        square,
        vector,
        turned,
        vector,
        vector,
        vector,
        square,
        vector,
        square,
        vector,
        vector,
        vector,
    )
    return jax.shard_map(local, mesh=mesh, in_specs=in_specs, out_specs=out_specs, check_vma=False)
```

```python
from functools import partial
import math

import jax
import jax.numpy as jnp
from jax import lax
from jax.experimental import pallas as pl
from jax.experimental.pallas import tpu as pltpu
from jax.sharding import PartitionSpec as P

HD = 64
EXTRA = 16
PIECES = 4


epsilon = 1e-05
masked = -1e30
low = jnp.bfloat16
SCALE = 1.0 / math.sqrt(HD)


def dot_nn(a, b):
    return lax.dot_general(a, b, (((1,), (0,)), ((), ())), preferred_element_type=jnp.float32)


def dot_tn(a, b):
    return lax.dot_general(a, b, (((0,), (0,)), ((), ())), preferred_element_type=jnp.float32)


def dot_nt(a, b):
    return lax.dot_general(a, b, (((1,), (1,)), ((), ())), preferred_element_type=jnp.float32)


def extra_rows(width, rows):
    index = lax.broadcasted_iota(jnp.int32, (EXTRA, width), 0)
    total = jnp.zeros((EXTRA, width), jnp.float32)
    for at, row in enumerate(rows):
        total = jnp.where(index == at, row, total)
    return total.astype(low)


def three_terms(row):
    high = row.astype(low).astype(jnp.float32)
    rest = row - high
    mid = rest.astype(low).astype(jnp.float32)
    return [high, mid, rest - mid]


def key_bias(keys, limit):
    position = lax.broadcasted_iota(jnp.int32, (1, keys), 1)
    return jnp.where(position < limit, 0.0, masked)


def attend_kernel(step, lens, q_ref, k_ref, v_ref, o_ref, lse_ref):
    queries, keys = q_ref.shape[1], k_ref.shape[1]
    one = jnp.ones((1, 1), jnp.float32)
    bias = key_bias(keys, lens[pl.program_id(0)])
    key_side = jnp.concatenate([k_ref[...], extra_rows(keys, [bias])], axis=0)
    value_side = jnp.concatenate([v_ref[...], extra_rows(keys, [one])], axis=0)
    for start in range(0, queries, step):
        part = pl.ds(start, step)
        query_side = jnp.concatenate([q_ref[:, part] * SCALE, extra_rows(step, [one])], axis=0)
        scores = dot_tn(key_side, query_side)
        peak = jnp.max(scores, axis=0, keepdims=True)
        probs = jnp.exp(scores - peak).astype(low)
        mixed = dot_nn(value_side, probs)
        total = mixed[HD : HD + 1]
        o_ref[:, part] = (mixed[:HD] / total).astype(low)
        lse_ref[0, :, part] = peak + jnp.log(total)


def attend_back_kernel(step, lens, q_ref, k_ref, v_ref, o_ref, lse_ref, g_ref, dq_ref, dk_ref, dv_ref, dk_sum, dv_sum):
    queries, keys = q_ref.shape[1], k_ref.shape[1]
    one = jnp.ones((1, 1), jnp.float32)
    bias = key_bias(keys, lens[pl.program_id(0)])
    key_side = jnp.concatenate([k_ref[...], extra_rows(keys, [bias, one, one, one])], axis=0)
    value_side = jnp.concatenate([v_ref[...], extra_rows(keys, [one, one, one])], axis=0)
    for start in range(0, queries, step):
        part = pl.ds(start, step)
        query, grad = q_ref[:, part] * SCALE, g_ref[:, part]
        delta = jnp.sum(
            grad.astype(jnp.float32) * o_ref[:, part].astype(jnp.float32), axis=0, keepdims=True
        )
        query_side = jnp.concatenate(
            [query, extra_rows(step, [one] + three_terms(-lse_ref[0, :, part]))], axis=0
        )
        grad_side = jnp.concatenate([grad, extra_rows(step, three_terms(-delta))], axis=0)
        probs = jnp.exp(dot_tn(key_side, query_side))
        grad_scores = (probs * dot_tn(value_side, grad_side)).astype(low)
        dq_ref[:, part] = (dot_nn(k_ref[...], grad_scores) * SCALE).astype(low)
        dk_part = dot_nt(query, grad_scores)
        dv_part = dot_nt(grad, probs.astype(low))
        if start == 0:
            dk_sum[...] = dk_part
            dv_sum[...] = dv_part
        else:
            dk_sum[...] += dk_part
            dv_sum[...] += dv_part
    dk_ref[...] = dk_sum[...].astype(low)
    dv_ref[...] = dv_sum[...].astype(low)


def query_step(queries, keys):
    for step in (256, 128):
        if queries % step == 0 and step * keys <= 2**20:
            return step
    return queries


def attention(lengths, q, k, v, count):
    return attention_part(lengths, q, k, v, count, 0, 1)


def attention_part(lengths, q, k, v, count, at, pieces):
    rows, tokens = q.shape
    queries, keys = tokens // count, k.shape[1] // count
    rows = rows // pieces
    heads = rows // HD
    begin = at * heads
    step = query_step(queries, keys)
    spec = lambda size: pl.BlockSpec((HD, size), lambda b, h, lens: (h + begin, b))
    out_spec = pl.BlockSpec((HD, queries), lambda b, h, lens: (h, b))
    return pl.pallas_call(
        partial(attend_kernel, step),
        grid_spec=pltpu.PrefetchScalarGridSpec(
            num_scalar_prefetch=1,
            grid=(count, heads),
            in_specs=[spec(queries), spec(keys), spec(keys)],
            out_specs=[out_spec, pl.BlockSpec((1, 1, queries), lambda b, h, lens: (h, 0, b))],
        ),
        out_shape=(
            jax.ShapeDtypeStruct((rows, tokens), low),
            jax.ShapeDtypeStruct((heads, 1, tokens), jnp.float32),
        ),
        cost_estimate=pl.CostEstimate(
            flops=16 * rows * tokens * keys,
            bytes_accessed=8 * rows * tokens,
            transcendentals=heads * tokens * keys,
        ),
        name="attend",
    )(lengths, q, k, v)


def attention_back(lengths, q, k, v, o, lse, grad, count):
    return attention_back_part(lengths, q, k, v, o, lse, grad, count, 0, 1)


def attention_back_part(lengths, q, k, v, o, lse, grad, count, at, pieces):
    rows, tokens = q.shape
    queries, keys = tokens // count, k.shape[1] // count
    rows = rows // pieces
    heads = rows // HD
    begin = at * heads
    step = query_step(queries, keys)
    spec = lambda size: pl.BlockSpec((HD, size), lambda b, h, lens: (h + begin, b))
    out_spec = lambda size: pl.BlockSpec((HD, size), lambda b, h, lens: (h, b))
    return pl.pallas_call(
        partial(attend_back_kernel, step),
        grid_spec=pltpu.PrefetchScalarGridSpec(
            num_scalar_prefetch=1,
            grid=(count, heads),
            in_specs=[
                spec(queries),
                spec(keys),
                spec(keys),
                spec(queries),
                pl.BlockSpec((1, 1, queries), lambda b, h, lens: (h + begin, 0, b)),
                spec(queries),
            ],
            out_specs=[out_spec(queries), out_spec(keys), out_spec(keys)],
            scratch_shapes=[pltpu.VMEM((HD, keys), jnp.float32)] * 2,
        ),
        out_shape=(
            jax.ShapeDtypeStruct((rows, tokens), low),
            jax.ShapeDtypeStruct((rows, k.shape[1]), low),
            jax.ShapeDtypeStruct((rows, k.shape[1]), low),
        ),
        cost_estimate=pl.CostEstimate(
            flops=40 * rows * tokens * keys,
            bytes_accessed=16 * rows * tokens,
            transcendentals=heads * tokens * keys,
        ),
        name="attend_back",
    )(lengths, q, k, v, o, lse, grad)


def piece_attend(length, qkv, mixed, at):
    full, tokens = qkv.shape[0] // 3, qkv.shape[1]
    heads = full // (4 * HD)
    step = query_step(tokens, tokens)
    base = (at // 2) * 6 * heads + (at % 2) * heads
    spec = lambda kind: pl.BlockSpec((HD, tokens), lambda b, h, lens: (base + 2 * kind * heads + h, 0))
    fresh = mixed is None

    def kernel(lens, q_ref, k_ref, v_ref, *refs):
        o_ref, lse_ref = refs[-2:]
        attend_kernel(step, lens, q_ref, k_ref, v_ref, o_ref, lse_ref)

    return pl.pallas_call(
        kernel,
        grid_spec=pltpu.PrefetchScalarGridSpec(
            num_scalar_prefetch=1,
            grid=(1, heads),
            in_specs=[spec(0), spec(1), spec(2)] + [pl.BlockSpec(memory_space=pl.ANY)] * (not fresh),
            out_specs=[
                pl.BlockSpec((HD, tokens), lambda b, h, lens: (at * heads + h, 0)),
                pl.BlockSpec((1, 1, tokens), lambda b, h, lens: (h, 0, 0)),
            ],
        ),
        out_shape=(
            jax.ShapeDtypeStruct((full, tokens), low),
            jax.ShapeDtypeStruct((heads, 1, tokens), jnp.float32),
        ),
        input_output_aliases={} if fresh else {4: 0},
        cost_estimate=pl.CostEstimate(
            flops=4 * full * tokens * tokens,
            bytes_accessed=2 * full * tokens,
            transcendentals=heads * tokens * tokens,
        ),
        name="attend",
    )(*((length, qkv, qkv, qkv) + (() if fresh else (mixed,))))


def piece_attend_back(length, qkv, mixed, lse, grad, dqkv, at):
    full, tokens = qkv.shape[0] // 3, qkv.shape[1]
    heads = full // (4 * HD)
    step = query_step(tokens, tokens)
    base = (at // 2) * 6 * heads + (at % 2) * heads
    spec = lambda kind: pl.BlockSpec((HD, tokens), lambda b, h, lens: (base + 2 * kind * heads + h, 0))
    mine = pl.BlockSpec((HD, tokens), lambda b, h, lens: (at * heads + h, 0))
    fresh = dqkv is None

    def kernel(lens, q_ref, k_ref, v_ref, o_ref, lse_ref, g_ref, *refs):
        d_ref, dk_sum, dv_sum = refs[-3:]
        attend_back_kernel(
            step,
            lens,
            q_ref,
            k_ref,
            v_ref,
            o_ref,
            lse_ref,
            g_ref,
            d_ref.at[0],
            d_ref.at[1],
            d_ref.at[2],
            dk_sum,
            dv_sum,
        )

    return pl.pallas_call(
        kernel,
        grid_spec=pltpu.PrefetchScalarGridSpec(
            num_scalar_prefetch=1,
            grid=(1, heads),
            in_specs=[
                spec(0),
                spec(1),
                spec(2),
                mine,
                pl.BlockSpec((1, 1, tokens), lambda b, h, lens: (h, 0, 0)),
                mine,
            ]
            + [pl.BlockSpec(memory_space=pl.ANY)] * (not fresh),
            out_specs=pl.BlockSpec((3, HD, tokens), lambda b, h, lens: (0, (at % 2) * heads + h, 0)),
            scratch_shapes=[pltpu.VMEM((HD, tokens), jnp.float32)] * 2,
        ),
        out_shape=jax.ShapeDtypeStruct((3, full // 2, tokens), low),
        input_output_aliases={} if fresh else {7: 0},
        cost_estimate=pl.CostEstimate(
            flops=10 * full * tokens * tokens,
            bytes_accessed=4 * full * tokens,
            transcendentals=heads * tokens * tokens,
        ),
        name="attend_back",
    )(*((length, qkv, qkv, qkv, mixed, lse, grad) + (() if fresh else (dqkv,))))


def up_form(weight, rows):
    product = jnp.einsum("cij,it->cjt", weight, rows, preferred_element_type=jnp.float32)
    return product.reshape(-1, rows.shape[1])


def down_form(weight, rows):
    rows = rows.reshape(weight.shape[0], weight.shape[2], rows.shape[1])
    return jnp.einsum("cij,cjt->it", weight, rows, preferred_element_type=jnp.float32)


def normalize(hidden, gain, shift):
    centre = jnp.mean(hidden, axis=0, keepdims=True)
    inverse = lax.rsqrt(jnp.mean(hidden * hidden, axis=0, keepdims=True) - centre * centre + epsilon)
    normed = (hidden - centre) * inverse
    return normed * gain + shift, normed, inverse


def norm_back(grad_out, normed, inverse, gain):
    scaled = grad_out * gain
    return inverse * (
        scaled
        - jnp.mean(scaled, axis=0, keepdims=True)
        - normed * jnp.mean(scaled * normed, axis=0, keepdims=True)
    )


def spread(piece):
    seqs, row, col = (lax.axis_size(name) for name in ("seqs", "row", "col"))
    height = piece.shape[0]
    if height % (16 * seqs) == 0:
        share = height // seqs
        piece = lax.dynamic_slice_in_dim(piece, lax.axis_index("seqs") * share, share, 0)
        whole = lax.all_gather(piece, ("col", "row", "seqs"), axis=0, tiled=True)
    else:
        whole = lax.all_gather(piece, ("col", "row"), axis=0, tiled=True)
    return whole.reshape(col, row * height, piece.shape[1])


def collect(grad):
    seqs = lax.axis_size("seqs")
    grad = lax.psum_scatter(grad.astype(low), "row", scatter_dimension=0, tiled=True)
    if grad.shape[0] % (16 * seqs) == 0:
        grad = lax.psum_scatter(grad, "seqs", scatter_dimension=0, tiled=True)
        grad = lax.psum_scatter(grad, "col", scatter_dimension=1, tiled=True)
        return lax.all_gather(grad, "seqs", axis=0, tiled=True)
    grad = lax.psum_scatter(grad, "col", scatter_dimension=1, tiled=True)
    return lax.psum(grad, "seqs")


def swap(array, axis, mask):
    size = lax.axis_size(axis)
    return lax.ppermute(array, axis, [(at, at ^ mask) for at in range(size)])


def add(*terms):
    return sum(term.astype(jnp.float32) for term in terms).astype(low)


def by_place(blocks, axis):
    own = lax.axis_index(axis)
    return jnp.stack([lax.dynamic_index_in_dim(blocks, own ^ at, 0, keepdims=False) for at in range(4)])


def fetch_steps(block):
    (block,) = yield [block]
    own = lax.dynamic_index_in_dim(block, lax.axis_index("seqs"), 0, keepdims=True)
    own = jnp.concatenate([own] + (yield [swap(own, "col", at) for at in (1, 2, 3)]), axis=0)
    *parts, own_row = yield [swap(own, "seqs", at) for at in (1, 2, 3)] + [swap(own, "row", 1)]
    rows = yield [swap(part, "row", 1) for part in parts]
    return [own] + parts + [own_row] + rows


def assemble(parts, out_shapes, moves):
    def kernel(*refs):
        ins, outs, done = refs[: len(parts)], refs[len(parts) : -1], refs[-1]
        copies = [
            pltpu.make_async_copy(ins[part].at[source], outs[out].at[target], done.at[at])
            for at, (part, source, out, target) in enumerate(moves)
        ]
        for copy in copies:
            copy.start()
        for copy in copies:
            copy.wait()

    return pl.pallas_call(
        kernel,
        in_specs=[pl.BlockSpec(memory_space=pl.ANY)] * len(parts),
        out_specs=[pl.BlockSpec(memory_space=pl.ANY)] * len(out_shapes),
        out_shape=[jax.ShapeDtypeStruct(shape, low) for shape in out_shapes],
        scratch_shapes=[pltpu.SemaphoreType.DMA((len(moves),))],
        name="assemble",
    )(*parts)


def assemble_units(parts):
    blocks, share, n = parts[0].shape
    every = slice(None)
    moves = [
        (at, (every, every, every), 0, (every, at % 4, every, pl.ds((at // 4) * n, n))) for at in range(8)
    ]
    (whole,) = assemble(parts, [(blocks, 4, share, 2 * n)], moves)
    return whole.reshape(4 * blocks * share, 2 * n)


def assemble_square(parts):
    width, n = parts[0].shape[1:]
    heads, deep = width // HD, HD // 4
    parts = [part.reshape(4, 4, heads, deep, n) for part in parts]
    every, moves = slice(None), []
    for at in range(8):
        lanes = pl.ds((at // 4) * n, n)
        for block in range(4):
            moves.append(
                (
                    at,
                    (block, pl.ds(0, 3), every, every, every),
                    0,
                    (block // 2, every, block % 2, every, at % 4, every, lanes),
                )
            )
            moves.append((at, (block, 3, every, every, every), 1, (block, every, at % 4, every, lanes)))
    shapes = [(2, 3, 2, heads, 4, deep, 2 * n), (4, heads, 4, deep, 2 * n)]
    qkv, out = assemble(parts, shapes, moves)
    return qkv.reshape(12 * width, 2 * n), out.reshape(4 * width, 2 * n)


def scaled_product(slope, weight, rows):
    units, full = weight.shape
    tokens = rows.shape[1]
    step = 512 if units % 512 == 0 else units

    def kernel(slope_ref, weight_ref, rows_ref, out_ref, sum_ref):
        product = dot_nn(weight_ref[...], rows_ref[...])
        product = (slope_ref[...].astype(jnp.float32) * product).astype(low)
        out_ref[...] = product
        sum_ref[...] = jnp.sum(product.astype(jnp.float32), axis=1, keepdims=True)

    return pl.pallas_call(
        kernel,
        grid=(units // step,),
        in_specs=[
            pl.BlockSpec((step, tokens), lambda at: (at, 0)),
            pl.BlockSpec((step, full), lambda at: (at, 0)),
            pl.BlockSpec((full, tokens), lambda at: (0, 0)),
        ],
        out_specs=[
            pl.BlockSpec((step, tokens), lambda at: (at, 0)),
            pl.BlockSpec((step, 1), lambda at: (at, 0)),
        ],
        out_shape=(
            jax.ShapeDtypeStruct((units, tokens), low),
            jax.ShapeDtypeStruct((units, 1), jnp.float32),
        ),
        cost_estimate=pl.CostEstimate(
            flops=2 * units * full * tokens,
            bytes_accessed=4 * units * tokens + 2 * units * full,
            transcendentals=0,
        ),
        name="scaled_product",
    )(slope, weight, rows)


def plane_steps(keep, send):
    keep, send = yield [keep, send]
    (got,) = yield [swap(send, "row", 1)]
    parts = [add(keep[:, at], got[:, at]) for at in range(4)]
    got = yield [swap(parts[at], "seqs", at) for at in (1, 2, 3)]
    return add(parts[0], *got)


def far_steps(keep, send):
    blocks = yield from plane_steps(keep, send)
    (got,) = yield [swap(blocks, "col", 2)]
    return got


def end_steps(own, far):
    (got,) = yield [swap(add(own[1], far[1]), "col", 1)]
    near = add(own[0], far[0], got)
    return by_place(jnp.stack([near] + (yield [swap(near, "seqs", at) for at in (1, 2, 3)])), "seqs")


def reduce_steps(keep, send):
    blocks = yield from plane_steps(keep, send)
    (far,) = yield [swap(blocks[2:], "col", 2)]
    return (yield from end_steps(blocks[:2], far))


def near_steps(keep, send, far):
    own = yield from plane_steps(keep, send)
    return (yield from end_steps(own, far.result))


def sum_steps(array):
    (array,) = yield [array]
    (got,) = yield [swap(array, "row", 1)]
    array = array + got
    array = sum((yield [swap(array, "seqs", at) for at in (1, 2, 3)]), array)
    return sum((yield [swap(array[at], "col", at) for at in (1, 2, 3)]), array[0])


class Chain:
    def __init__(self, steps):
        self.steps, self.result = steps, None
        self.flight = next(steps)

    def advance(self, flight):
        try:
            self.flight = self.steps.send(flight)
        except StopIteration as stop:
            self.flight, self.result = [], stop.value


def stage(main, *chains):
    chains = [chain for chain in chains if chain.result is None]
    main, flights = lax.optimization_barrier((main, [chain.flight for chain in chains]))
    for chain, flight in zip(chains, flights):
        chain.advance(flight)
    return main


def drain(*chains):
    while any(chain.result is None for chain in chains):
        stage(jnp.zeros((), jnp.float32), *chains)


def gelu_both(pre):
    size = jnp.abs(pre)
    bell = jnp.exp(-0.5 * (pre * pre))
    t = 1.0 / (1.0 + (0.3275911 * math.sqrt(0.5)) * size)
    tail = 0.5 * 1.061405429
    for term in (-1.453152027, 1.421413741, -0.284496736, 0.254829592):
        tail = tail * t + 0.5 * term
    tail = tail * t * bell
    phi = jnp.where(pre < 0.0, tail, 1.0 - tail)
    return pre * phi, phi + pre * bell * (1.0 / math.sqrt(2.0 * math.pi))


def local_fast(
    tokens,
    length,
    query_weight,
    query_bias,
    key_weight,
    value_weight,
    value_bias,
    out_weight,
    out_bias,
    first_gain,
    first_shift,
    up_weight,
    up_bias,
    down_weight,
    down_bias,
    second_gain,
    second_shift,
    cotangent,
):
    seq_count, width, slots = tokens.shape
    half = 2 * width
    full, count = 4 * width, 2 * slots
    units = up_weight.shape[1]
    row_at, col_at = lax.axis_index("row"), lax.axis_index("col")

    def turn(array):
        return jnp.where(row_at == 1, jnp.concatenate([array[half:], array[:half]], axis=0), array)

    def enter(array):
        array = lax.all_to_all(array, ("col", "row"), split_axis=0, concat_axis=0, tiled=True)
        array = array.reshape(4, 2, width, slots)
        array = jnp.concatenate([array[:, 0], array[:, 1]], axis=2)
        return turn(array.reshape(full, count))

    def arrange(array):
        array = turn(array).reshape(4, width, count)
        array = jnp.stack([array[:, :, :slots], array[:, :, slots:]], axis=1)
        return array.reshape(seq_count, width, slots)

    def leave(array):
        return lax.all_to_all(array, ("col", "row"), split_axis=0, concat_axis=0, tiled=True)

    def head_order(array):
        array = array.reshape(4, width // HD, 4, HD // 4, -1)
        return jnp.moveaxis(by_place(jnp.moveaxis(array, 2, 0), "seqs"), 0, 2).reshape(full, -1)

    def unit_order(array):
        array = array.reshape(4, 4, units // 4)
        return jnp.moveaxis(by_place(jnp.moveaxis(array, 1, 0), "seqs"), 0, 1).reshape(4 * units, 1)

    heads = width // HD
    square = [query_weight.T, key_weight.T, value_weight.T, out_weight]
    square = jnp.stack(square).astype(low).reshape(4, heads, 4, HD // 4, half)
    square = jnp.transpose(square, (2, 0, 1, 3, 4)).reshape(4, width, half)
    square = Chain(fetch_steps(square))
    up = Chain(fetch_steps(up_weight.T.astype(low).reshape(4, units // 4, half)))
    down = Chain(fetch_steps(down_weight.T.astype(low).reshape(4, units // 4, half)))

    small = [query_bias, value_bias, out_bias, first_gain, first_shift, down_bias, second_gain, second_shift]
    small = jnp.concatenate(small + [up_bias])
    small = stage(small, square)
    got = [swap(small, "col", at) for at in (1, 2, 3)]
    tokens, got = stage((tokens, got), square)
    x_low = enter(tokens)
    small = jnp.stack([small] + got)
    vectors = jnp.transpose(small[:, : 8 * width].reshape(4, 8, width), (0, 2, 1))
    bias = head_order(vectors[:, :, :2]).reshape(2, 2 * width, 2)
    bias = jnp.stack([bias[:, :, 0], jnp.zeros_like(bias[:, :, 0]), bias[:, :, 1]], axis=1).reshape(3 * full, 1)
    vectors = turn(by_place(vectors[:, :, 2:], "col").reshape(full, 6))
    vectors = [vectors[:, at : at + 1] for at in range(6)]
    ub = unit_order(small[:, 8 * width :])
    bias, vectors, ub = stage((bias, vectors, ub), square)
    stage((), square)
    qkv_full, out_full = assemble_square(square.result)
    x_low, qkv_full, out_full, bias, vectors, ub = stage((x_low, qkv_full, out_full, bias, vectors, ub), up)
    ob, gain1, shift1, db, gain2, shift2 = vectors

    qkv = (dot_nn(qkv_full, x_low) + bias).astype(low)
    mixed, lse = None, []
    for at, chains in enumerate(((), (up, down), (), (up, down))):
        if at == 3:
            qkv, mixed, cotangent = stage((qkv, mixed, cotangent), *chains)
        else:
            qkv, mixed = stage((qkv, mixed), *chains)
        mixed, part = piece_attend(length, qkv, mixed, at)
        lse.append(part)
    g = lax.optimization_barrier(enter(cotangent))
    mixed = stage(mixed, up)
    h1 = x_low.astype(jnp.float32) + (dot_tn(out_full, mixed) + ob)
    y1, n1, inv1 = normalize(h1, gain1, shift1)
    y1_low = stage(y1.astype(low), down)
    up_full = assemble_units(up.result)
    act, slope = gelu_both(dot_nn(up_full, y1_low) + ub)
    act_low, slope = stage((act.astype(low), slope.astype(low)), down)
    down_full = assemble_units(down.result)
    h2 = y1 + (dot_tn(down_full, act_low) + db)
    out, n2, inv2 = normalize(h2, gain2, shift2)
    layer_output = leave(arrange(out.astype(low)))

    ones = jnp.ones((count, 128), low)
    token_sum = lambda array: dot_nn(array, ones)[:, 0]
    valid = (jnp.arange(count, dtype=jnp.int32)[None, :] < length[:, None]).astype(jnp.float32)
    g = g.astype(jnp.float32) * valid
    gain2_grad = jnp.sum(g * n2, axis=1)
    shift2_grad = jnp.sum(g, axis=1)
    dh2 = norm_back(g, n2, inv2, gain2)
    dz = dh2.astype(low)
    db_grad = token_sum(dz)
    by_share = lambda grad: grad.astype(low).reshape(4, 4, units // 4, half)

    def halves(one, two):
        return by_share(dot_nt(one, two[:half])), by_share(dot_nt(one, two[half:]))

    down_grad = Chain(reduce_steps(*halves(act_low, dz)))
    dz = stage(dz, down_grad)
    dpre, ub_grad = scaled_product(slope, down_full, dz)
    dpre = stage(dpre, down_grad)
    up_grad = Chain(reduce_steps(*halves(dpre, y1_low)))
    dpre = stage(dpre, up_grad)
    dy1 = dh2 + dot_tn(up_full, dpre)
    gain1_grad = jnp.sum(dy1 * n1, axis=1)
    shift1_grad = jnp.sum(dy1, axis=1)
    dh1 = norm_back(dy1, n1, inv1, gain1)
    da = dh1.astype(low)
    da = stage(da)
    ob_grad = token_sum(da)
    out_grad = [dot_nt(mixed, part).astype(low) for part in (da[:half], da[half:])]
    grad_mixed = dot_nn(out_full, da).astype(low)
    grad_mixed, out_grad = stage((grad_mixed, out_grad), up_grad)

    def square_share(pair, dqkv):
        rows = dqkv.reshape(6 * width, count)
        shares = []
        for part, other in zip((x_low[:half], x_low[half:]), out_grad):
            grad = dot_nt(rows, part).astype(low).reshape(3, 2 * width, half)
            other = other[2 * width * pair : 2 * width * (pair + 1)]
            grad = jnp.concatenate([grad, other[None]], axis=0).reshape(4, 2, heads, 4, HD // 4, half)
            shares.append(jnp.transpose(grad, (1, 3, 0, 2, 4, 5)).reshape(2, 4, width, half))
        return shares

    dqkv = piece_attend_back(length, qkv, mixed, lse[2], grad_mixed, None, 2)
    grad_mixed, dqkv = stage((grad_mixed, dqkv), down_grad)
    dqkv = piece_attend_back(length, qkv, mixed, lse[3], grad_mixed, dqkv, 3)
    grad_mixed, dqkv, layer_output = stage((grad_mixed, dqkv, layer_output), down_grad)
    far = Chain(far_steps(*square_share(1, dqkv)))
    dx = dh1 + dot_tn(qkv_full[6 * width :], dqkv.reshape(6 * width, count))
    v_sums = [token_sum(dqkv[2])]
    q_sums = [token_sum(dqkv[0])]
    by_col = lambda parts: jnp.transpose(jnp.concatenate(parts, axis=1).reshape(4, width, -1), (0, 2, 1))
    vectors = turn(jnp.stack([ob_grad, gain1_grad, shift1_grad, db_grad, gain2_grad, shift2_grad], axis=1))
    vectors = by_col([by_place(vectors.reshape(4, width, 6), "col").reshape(full, 6)]).reshape(4, 6 * width)
    ub_grad = unit_order(ub_grad.reshape(4, units)).reshape(4, units)
    early = jnp.concatenate([vectors, ub_grad], axis=1)
    grad_mixed, dx, v_sums, q_sums, early = stage(
        (grad_mixed, dx, v_sums, q_sums, early), far, up_grad, down_grad
    )
    dqkv = piece_attend_back(length, qkv, mixed, lse[0], grad_mixed, None, 0)
    grad_mixed, dqkv = stage((grad_mixed, dqkv), far, up_grad)
    dqkv = piece_attend_back(length, qkv, mixed, lse[1], grad_mixed, dqkv, 1)
    dqkv = stage(dqkv, up_grad, down_grad)
    square_grad = Chain(near_steps(*square_share(0, dqkv), far))
    dqkv, dx = stage((dqkv, dx), square_grad, far)
    dx = dx + dot_tn(qkv_full[: 6 * width], dqkv.reshape(6 * width, count))
    dx, dqkv = stage((arrange(dx.astype(low)), dqkv), square_grad, far, up_grad)
    tokens_grad = leave(dx)
    v_sums = jnp.concatenate([token_sum(dqkv[2])] + v_sums)
    q_sums = jnp.concatenate([token_sum(dqkv[0])] + q_sums)
    late = head_order(jnp.stack([q_sums, v_sums], axis=1).reshape(4, width, 2))
    late = by_col([late]).reshape(4, 2 * width)
    small_grad = Chain(sum_steps(jnp.concatenate([late, early], axis=1)))
    drain(square_grad, far, up_grad, small_grad)

    small_grad = small_grad.result
    pieces = [small_grad[at * width : (at + 1) * width] for at in range(8)]
    square_grad = square_grad.result.reshape(4, 4, heads, HD // 4, half)
    square_grad = jnp.transpose(square_grad, (1, 2, 0, 3, 4)).reshape(4, width, half).astype(jnp.float32)
    block = lambda grad: grad.result.reshape(units, half).astype(jnp.float32).T
    return (
        layer_output,
        tokens_grad,
        square_grad[0].T,
        pieces[0],
        square_grad[1].T,
        square_grad[2].T,
        pieces[1],
        square_grad[3],
        pieces[2],
        pieces[3],
        pieces[4],
        block(up_grad),
        small_grad[8 * width :],
        block(down_grad),
        pieces[5],
        pieces[6],
        pieces[7],
    )


def local(
    tokens,
    lengths,
    query_weight,
    query_bias,
    key_weight,
    value_weight,
    value_bias,
    out_weight,
    out_bias,
    first_gain,
    first_shift,
    up_weight,
    up_bias,
    down_weight,
    down_bias,
    second_gain,
    second_shift,
    cotangent,
):
    seq_count, width, rows = tokens.shape
    row, col = lax.axis_size("row"), lax.axis_size("col")
    row_at, col_at = lax.axis_index("row"), lax.axis_index("col")
    members = row * col
    full = width * col
    alone = seq_count % members == 0
    if alone:
        count = seq_count // members
        mine = row * rows
        first = jnp.int32(0)
        own_lengths = lax.dynamic_slice_in_dim(lengths, (col_at * row + row_at) * count, count, 0)
    else:
        count = seq_count // col
        mine = rows
        first = row_at * rows
        own_lengths = lax.dynamic_slice_in_dim(lengths, col_at * count, count, 0)

    def enter(array):
        if alone:
            array = lax.all_to_all(array, ("col", "row"), split_axis=0, concat_axis=0, tiled=True)
            array = array.reshape(col, row, count, width, rows)
            return jnp.transpose(array, (0, 3, 2, 1, 4)).reshape(full, count * mine)
        array = lax.all_to_all(array, "col", split_axis=0, concat_axis=0, tiled=True)
        array = array.reshape(col, count, width, rows)
        return jnp.transpose(array, (0, 2, 1, 3)).reshape(full, count * mine)

    def leave(array):
        if alone:
            array = array.reshape(col, width, count, row, rows)
            array = jnp.transpose(array, (0, 3, 2, 1, 4)).reshape(seq_count, width, rows)
            return lax.all_to_all(array, ("col", "row"), split_axis=0, concat_axis=0, tiled=True)
        array = jnp.transpose(array.reshape(col, width, count, mine), (0, 2, 1, 3))
        array = array.reshape(seq_count, width, rows)
        return lax.all_to_all(array, "col", split_axis=0, concat_axis=0, tiled=True)

    if alone and lax.axis_size("seqs") == 4 and row == 2 and col == 4 and count == 1 and width == 3 * HD:
        return local_fast(
            tokens,
            own_lengths,
            query_weight,
            query_bias,
            key_weight,
            value_weight,
            value_bias,
            out_weight,
            out_bias,
            first_gain,
            first_shift,
            up_weight,
            up_bias,
            down_weight,
            down_bias,
            second_gain,
            second_shift,
            cotangent,
        )

    def by_sequence(move, array):
        parts = [move(part) for part in jnp.split(array, count, axis=1)]
        return jnp.concatenate(parts, axis=1)

    def all_keys(array):
        if alone:
            return array
        return by_sequence(lambda part: lax.all_gather(part, "row", axis=1, tiled=True), array)

    def own_keys(array):
        if alone:
            return array
        return by_sequence(
            lambda part: lax.psum_scatter(part, "row", scatter_dimension=1, tiled=True), array
        )

    x_low = enter(tokens)
    qkv_piece = jnp.concatenate([query_weight, key_weight, value_weight], axis=1).astype(low)
    qkv_full = spread(qkv_piece)
    out_full = spread(out_weight.T.astype(low))
    up_full = spread(up_weight.astype(low))
    down_full = spread(down_weight.astype(low))
    small = jnp.concatenate(
        [
            query_bias,
            value_bias,
            out_bias,
            first_gain,
            first_shift,
            down_bias,
            second_gain,
            second_shift,
            up_bias,
        ]
    )
    small = lax.all_gather(small, "col", axis=0, tiled=False)
    vectors = [small[:, at * width : (at + 1) * width].reshape(full, 1) for at in range(8)]
    qb, vb, ob, gain1, shift1, db, gain2, shift2 = vectors
    ub = small[:, 8 * width :].reshape(-1, 1)

    token_count = count * mine
    qkv = up_form(qkv_full, x_low).reshape(col, 3, width, token_count)
    q = (qkv[:, 0].reshape(full, token_count) + qb).astype(low)
    k = qkv[:, 1].reshape(full, token_count).astype(low)
    v = (qkv[:, 2].reshape(full, token_count) + vb).astype(low)
    k_all, v_all = all_keys(k), all_keys(v)
    mixed, lse = attention(own_lengths, q, k_all, v_all, count)
    h1 = x_low.astype(jnp.float32) + (down_form(out_full, mixed) + ob)
    y1, n1, inv1 = normalize(h1, gain1, shift1)
    y1_low = y1.astype(low)
    pre = up_form(up_full, y1_low) + ub
    act, gelu_back = jax.vjp(partial(jax.nn.gelu, approximate=False), pre)
    act_low = act.astype(low)
    h2 = y1 + (down_form(down_full, act_low) + db)
    out, n2, inv2 = normalize(h2, gain2, shift2)
    layer_output = leave(out.astype(low))

    position = first + jnp.arange(mine, dtype=jnp.int32)
    valid = (position[None, :] < own_lengths[:, None]).astype(jnp.float32).reshape(1, token_count)
    g = enter(cotangent).astype(jnp.float32) * valid
    gain2_grad = jnp.sum(g * n2, axis=1)
    shift2_grad = jnp.sum(g, axis=1)
    dh2 = norm_back(g, n2, inv2, gain2)
    dz = dh2.astype(low)
    db_grad = jnp.sum(dz, axis=1, dtype=jnp.float32)
    down_grad = collect(dot_nt(dz, act_low))
    dpre = gelu_back(up_form(down_full, dz))[0].astype(low)
    ub_grad = jnp.sum(dpre, axis=1, dtype=jnp.float32)
    up_grad = collect(dot_nt(y1_low, dpre))
    dy1 = dh2 + down_form(up_full, dpre)
    gain1_grad = jnp.sum(dy1 * n1, axis=1)
    shift1_grad = jnp.sum(dy1, axis=1)
    dh1 = norm_back(dy1, n1, inv1, gain1)
    da = dh1.astype(low)
    ob_grad = jnp.sum(da, axis=1, dtype=jnp.float32)
    out_grad = collect(dot_nt(da, mixed))
    grad_mixed = up_form(out_full, da).astype(low)
    dq, dk, dv = attention_back(own_lengths, q, k_all, v_all, mixed, lse, grad_mixed, count)
    dk, dv = own_keys(dk), own_keys(dv)
    qb_grad = jnp.sum(dq, axis=1, dtype=jnp.float32)
    vb_grad = jnp.sum(dv, axis=1, dtype=jnp.float32)
    block = lambda array: array.reshape(col, width, token_count)
    dqkv = jnp.stack([block(dq), block(dk), block(dv)], axis=1).reshape(3 * full, token_count)
    dx = dh1 + down_form(qkv_full, dqkv)
    tokens_grad = leave(dx.astype(low))
    qkv_grad = collect(dot_nt(x_low, dqkv)).astype(jnp.float32)
    vectors = [qb_grad, vb_grad, ob_grad, gain1_grad, shift1_grad, db_grad, gain2_grad, shift2_grad]
    vectors = [vector.reshape(col, width) for vector in vectors] + [ub_grad.reshape(col, -1)]
    small_grad = lax.psum(jnp.concatenate(vectors, axis=1), ("seqs", "row", "col"))
    small_grad = lax.dynamic_index_in_dim(small_grad, col_at, 0, keepdims=False)
    pieces = [small_grad[at * width : (at + 1) * width] for at in range(8)]
    return (
        layer_output,
        tokens_grad,
        qkv_grad[:, :width],
        pieces[0],
        qkv_grad[:, width : 2 * width],
        qkv_grad[:, 2 * width :],
        pieces[1],
        out_grad.astype(jnp.float32).T,
        pieces[2],
        pieces[3],
        pieces[4],
        up_grad.astype(jnp.float32),
        small_grad[8 * width :],
        down_grad.astype(jnp.float32),
        pieces[5],
        pieces[6],
        pieces[7],
    )


def solution(mesh):
    wide, vector = P("seqs", "col", "row"), P("col")
    square, turned = P("row", "col"), P("col", "row")
    in_specs = (
        wide,
        P("seqs"),
        square,
        vector,
        square,
        square,
        vector,
        turned,
        vector,
        vector,
        vector,
        square,
        vector,
        square,
        vector,
        vector,
        vector,
        wide,
    )
    out_specs = (
        wide,
        wide,
        square,
        vector,
        square,
        square,
        vector,
        turned,
        vector,
        vector,
        vector,
        square,
        vector,
        square,
        vector,
        vector,
        vector,
    )
    return jax.shard_map(local, mesh=mesh, in_specs=in_specs, out_specs=out_specs, check_vma=False)
```

```python
from functools import partial
import math

import jax
import jax.numpy as jnp
from jax import lax
from jax.experimental import pallas as pl
from jax.experimental.pallas import tpu as pltpu
from jax.sharding import PartitionSpec as P

HD = 64
EXTRA = 16
PIECES = 4


epsilon = 1e-05
masked = -1e30
low = jnp.bfloat16
SCALE = 1.0 / math.sqrt(HD)


def dot_nn(a, b):
    return lax.dot_general(a, b, (((1,), (0,)), ((), ())), preferred_element_type=jnp.float32)


def dot_tn(a, b):
    return lax.dot_general(a, b, (((0,), (0,)), ((), ())), preferred_element_type=jnp.float32)


def dot_nt(a, b):
    return lax.dot_general(a, b, (((1,), (1,)), ((), ())), preferred_element_type=jnp.float32)


def extra_rows(width, rows):
    index = lax.broadcasted_iota(jnp.int32, (EXTRA, width), 0)
    total = jnp.zeros((EXTRA, width), jnp.float32)
    for at, row in enumerate(rows):
        total = jnp.where(index == at, row, total)
    return total.astype(low)


def three_terms(row):
    high = row.astype(low).astype(jnp.float32)
    rest = row - high
    mid = rest.astype(low).astype(jnp.float32)
    return [high, mid, rest - mid]


def key_bias(keys, limit):
    position = lax.broadcasted_iota(jnp.int32, (1, keys), 1)
    return jnp.where(position < limit, 0.0, masked)


def attend_kernel(step, lens, q_ref, k_ref, v_ref, o_ref, lse_ref):
    queries, keys = q_ref.shape[1], k_ref.shape[1]
    one = jnp.ones((1, 1), jnp.float32)
    bias = key_bias(keys, lens[pl.program_id(0)])
    key_side = jnp.concatenate([k_ref[...], extra_rows(keys, [bias])], axis=0)
    value_side = jnp.concatenate([v_ref[...], extra_rows(keys, [one])], axis=0)
    for start in range(0, queries, step):
        part = pl.ds(start, step)
        query_side = jnp.concatenate([q_ref[:, part] * SCALE, extra_rows(step, [one])], axis=0)
        scores = dot_tn(key_side, query_side)
        peak = jnp.max(scores, axis=0, keepdims=True)
        probs = jnp.exp(scores - peak).astype(low)
        mixed = dot_nn(value_side, probs)
        total = mixed[HD : HD + 1]
        o_ref[:, part] = (mixed[:HD] / total).astype(low)
        lse_ref[0, :, part] = peak + jnp.log(total)


def attend_back_kernel(step, lens, q_ref, k_ref, v_ref, o_ref, lse_ref, g_ref, dq_ref, dk_ref, dv_ref, dk_sum, dv_sum):
    queries, keys = q_ref.shape[1], k_ref.shape[1]
    one = jnp.ones((1, 1), jnp.float32)
    bias = key_bias(keys, lens[pl.program_id(0)])
    key_side = jnp.concatenate([k_ref[...], extra_rows(keys, [bias, one, one, one])], axis=0)
    value_side = jnp.concatenate([v_ref[...], extra_rows(keys, [one, one, one])], axis=0)
    for start in range(0, queries, step):
        part = pl.ds(start, step)
        query, grad = q_ref[:, part] * SCALE, g_ref[:, part]
        delta = jnp.sum(
            grad.astype(jnp.float32) * o_ref[:, part].astype(jnp.float32), axis=0, keepdims=True
        )
        query_side = jnp.concatenate(
            [query, extra_rows(step, [one] + three_terms(-lse_ref[0, :, part]))], axis=0
        )
        grad_side = jnp.concatenate([grad, extra_rows(step, three_terms(-delta))], axis=0)
        probs = jnp.exp(dot_tn(key_side, query_side))
        grad_scores = (probs * dot_tn(value_side, grad_side)).astype(low)
        dq_ref[:, part] = (dot_nn(k_ref[...], grad_scores) * SCALE).astype(low)
        dk_part = dot_nt(query, grad_scores)
        dv_part = dot_nt(grad, probs.astype(low))
        if start == 0:
            dk_sum[...] = dk_part
            dv_sum[...] = dv_part
        else:
            dk_sum[...] += dk_part
            dv_sum[...] += dv_part
    dk_ref[...] = dk_sum[...].astype(low)
    dv_ref[...] = dv_sum[...].astype(low)


def query_step(queries, keys):
    for step in (256, 128):
        if queries % step == 0 and step * keys <= 2**20:
            return step
    return queries


def attention(lengths, q, k, v, count):
    return attention_part(lengths, q, k, v, count, 0, 1)


def attention_part(lengths, q, k, v, count, at, pieces):
    rows, tokens = q.shape
    queries, keys = tokens // count, k.shape[1] // count
    rows = rows // pieces
    heads = rows // HD
    begin = at * heads
    step = query_step(queries, keys)
    spec = lambda size: pl.BlockSpec((HD, size), lambda b, h, lens: (h + begin, b))
    out_spec = pl.BlockSpec((HD, queries), lambda b, h, lens: (h, b))
    return pl.pallas_call(
        partial(attend_kernel, step),
        grid_spec=pltpu.PrefetchScalarGridSpec(
            num_scalar_prefetch=1,
            grid=(count, heads),
            in_specs=[spec(queries), spec(keys), spec(keys)],
            out_specs=[out_spec, pl.BlockSpec((1, 1, queries), lambda b, h, lens: (h, 0, b))],
        ),
        out_shape=(
            jax.ShapeDtypeStruct((rows, tokens), low),
            jax.ShapeDtypeStruct((heads, 1, tokens), jnp.float32),
        ),
        cost_estimate=pl.CostEstimate(
            flops=16 * rows * tokens * keys,
            bytes_accessed=8 * rows * tokens,
            transcendentals=heads * tokens * keys,
        ),
        name="attend",
    )(lengths, q, k, v)


def attention_back(lengths, q, k, v, o, lse, grad, count):
    return attention_back_part(lengths, q, k, v, o, lse, grad, count, 0, 1)


def attention_back_part(lengths, q, k, v, o, lse, grad, count, at, pieces):
    rows, tokens = q.shape
    queries, keys = tokens // count, k.shape[1] // count
    rows = rows // pieces
    heads = rows // HD
    begin = at * heads
    step = query_step(queries, keys)
    spec = lambda size: pl.BlockSpec((HD, size), lambda b, h, lens: (h + begin, b))
    out_spec = lambda size: pl.BlockSpec((HD, size), lambda b, h, lens: (h, b))
    return pl.pallas_call(
        partial(attend_back_kernel, step),
        grid_spec=pltpu.PrefetchScalarGridSpec(
            num_scalar_prefetch=1,
            grid=(count, heads),
            in_specs=[
                spec(queries),
                spec(keys),
                spec(keys),
                spec(queries),
                pl.BlockSpec((1, 1, queries), lambda b, h, lens: (h + begin, 0, b)),
                spec(queries),
            ],
            out_specs=[out_spec(queries), out_spec(keys), out_spec(keys)],
            scratch_shapes=[pltpu.VMEM((HD, keys), jnp.float32)] * 2,
        ),
        out_shape=(
            jax.ShapeDtypeStruct((rows, tokens), low),
            jax.ShapeDtypeStruct((rows, k.shape[1]), low),
            jax.ShapeDtypeStruct((rows, k.shape[1]), low),
        ),
        cost_estimate=pl.CostEstimate(
            flops=40 * rows * tokens * keys,
            bytes_accessed=16 * rows * tokens,
            transcendentals=heads * tokens * keys,
        ),
        name="attend_back",
    )(lengths, q, k, v, o, lse, grad)


def piece_attend(length, qkv, mixed, at):
    full, tokens = qkv.shape[0] // 3, qkv.shape[1]
    heads = full // (4 * HD)
    step = query_step(tokens, tokens)
    base = (at // 2) * 6 * heads + (at % 2) * heads
    spec = lambda kind: pl.BlockSpec((HD, tokens), lambda b, h, lens: (base + 2 * kind * heads + h, 0))
    fresh = mixed is None

    def kernel(lens, q_ref, k_ref, v_ref, *refs):
        o_ref, lse_ref = refs[-2:]
        attend_kernel(step, lens, q_ref, k_ref, v_ref, o_ref, lse_ref)

    return pl.pallas_call(
        kernel,
        grid_spec=pltpu.PrefetchScalarGridSpec(
            num_scalar_prefetch=1,
            grid=(1, heads),
            in_specs=[spec(0), spec(1), spec(2)] + [pl.BlockSpec(memory_space=pl.ANY)] * (not fresh),
            out_specs=[
                pl.BlockSpec((HD, tokens), lambda b, h, lens: (at * heads + h, 0)),
                pl.BlockSpec((1, 1, tokens), lambda b, h, lens: (h, 0, 0)),
            ],
        ),
        out_shape=(
            jax.ShapeDtypeStruct((full, tokens), low),
            jax.ShapeDtypeStruct((heads, 1, tokens), jnp.float32),
        ),
        input_output_aliases={} if fresh else {4: 0},
        cost_estimate=pl.CostEstimate(
            flops=4 * full * tokens * tokens,
            bytes_accessed=2 * full * tokens,
            transcendentals=heads * tokens * tokens,
        ),
        name="attend",
    )(*((length, qkv, qkv, qkv) + (() if fresh else (mixed,))))


def piece_attend_back(length, qkv, mixed, lse, grad, dqkv, at):
    full, tokens = qkv.shape[0] // 3, qkv.shape[1]
    heads = full // (4 * HD)
    step = query_step(tokens, tokens)
    base = (at // 2) * 6 * heads + (at % 2) * heads
    spec = lambda kind: pl.BlockSpec((HD, tokens), lambda b, h, lens: (base + 2 * kind * heads + h, 0))
    mine = pl.BlockSpec((HD, tokens), lambda b, h, lens: (at * heads + h, 0))
    fresh = dqkv is None

    def kernel(lens, q_ref, k_ref, v_ref, o_ref, lse_ref, g_ref, *refs):
        d_ref, dk_sum, dv_sum = refs[-3:]
        attend_back_kernel(
            step,
            lens,
            q_ref,
            k_ref,
            v_ref,
            o_ref,
            lse_ref,
            g_ref,
            d_ref.at[0],
            d_ref.at[1],
            d_ref.at[2],
            dk_sum,
            dv_sum,
        )

    return pl.pallas_call(
        kernel,
        grid_spec=pltpu.PrefetchScalarGridSpec(
            num_scalar_prefetch=1,
            grid=(1, heads),
            in_specs=[
                spec(0),
                spec(1),
                spec(2),
                mine,
                pl.BlockSpec((1, 1, tokens), lambda b, h, lens: (h, 0, 0)),
                mine,
            ]
            + [pl.BlockSpec(memory_space=pl.ANY)] * (not fresh),
            out_specs=pl.BlockSpec((3, HD, tokens), lambda b, h, lens: (0, (at % 2) * heads + h, 0)),
            scratch_shapes=[pltpu.VMEM((HD, tokens), jnp.float32)] * 2,
        ),
        out_shape=jax.ShapeDtypeStruct((3, full // 2, tokens), low),
        input_output_aliases={} if fresh else {7: 0},
        cost_estimate=pl.CostEstimate(
            flops=10 * full * tokens * tokens,
            bytes_accessed=4 * full * tokens,
            transcendentals=heads * tokens * tokens,
        ),
        name="attend_back",
    )(*((length, qkv, qkv, qkv, mixed, lse, grad) + (() if fresh else (dqkv,))))


def up_form(weight, rows):
    product = jnp.einsum("cij,it->cjt", weight, rows, preferred_element_type=jnp.float32)
    return product.reshape(-1, rows.shape[1])


def down_form(weight, rows):
    rows = rows.reshape(weight.shape[0], weight.shape[2], rows.shape[1])
    return jnp.einsum("cij,cjt->it", weight, rows, preferred_element_type=jnp.float32)


def normalize(hidden, gain, shift):
    centre = jnp.mean(hidden, axis=0, keepdims=True)
    inverse = lax.rsqrt(jnp.mean(hidden * hidden, axis=0, keepdims=True) - centre * centre + epsilon)
    normed = (hidden - centre) * inverse
    return normed * gain + shift, normed, inverse


def norm_back(grad_out, normed, inverse, gain):
    scaled = grad_out * gain
    return inverse * (
        scaled
        - jnp.mean(scaled, axis=0, keepdims=True)
        - normed * jnp.mean(scaled * normed, axis=0, keepdims=True)
    )


def spread(piece):
    seqs, row, col = (lax.axis_size(name) for name in ("seqs", "row", "col"))
    height = piece.shape[0]
    if height % (16 * seqs) == 0:
        share = height // seqs
        piece = lax.dynamic_slice_in_dim(piece, lax.axis_index("seqs") * share, share, 0)
        whole = lax.all_gather(piece, ("col", "row", "seqs"), axis=0, tiled=True)
    else:
        whole = lax.all_gather(piece, ("col", "row"), axis=0, tiled=True)
    return whole.reshape(col, row * height, piece.shape[1])


def collect(grad):
    seqs = lax.axis_size("seqs")
    grad = lax.psum_scatter(grad.astype(low), "row", scatter_dimension=0, tiled=True)
    if grad.shape[0] % (16 * seqs) == 0:
        grad = lax.psum_scatter(grad, "seqs", scatter_dimension=0, tiled=True)
        grad = lax.psum_scatter(grad, "col", scatter_dimension=1, tiled=True)
        return lax.all_gather(grad, "seqs", axis=0, tiled=True)
    grad = lax.psum_scatter(grad, "col", scatter_dimension=1, tiled=True)
    return lax.psum(grad, "seqs")


def swap(array, axis, mask):
    size = lax.axis_size(axis)
    return lax.ppermute(array, axis, [(at, at ^ mask) for at in range(size)])


def add(*terms):
    return sum(term.astype(jnp.float32) for term in terms).astype(low)


def by_place(blocks, axis):
    own = lax.axis_index(axis)
    return jnp.stack([lax.dynamic_index_in_dim(blocks, own ^ at, 0, keepdims=False) for at in range(4)])


def fetch_steps(block):
    (block,) = yield [block]
    own = lax.dynamic_index_in_dim(block, lax.axis_index("seqs"), 0, keepdims=True)
    own = jnp.concatenate([own] + (yield [swap(own, "col", at) for at in (1, 2, 3)]), axis=0)
    *parts, own_row = yield [swap(own, "seqs", at) for at in (1, 2, 3)] + [swap(own, "row", 1)]
    rows = yield [swap(part, "row", 1) for part in parts]
    return [own] + parts + [own_row] + rows


def assemble_units(parts):
    blocks, share, n = parts[0].shape

    def kernel(*refs):
        for at in range(8):
            refs[8][0, at % 4, :, pl.ds((at // 4) * n, n)] = refs[at][0]

    whole = pl.pallas_call(
        kernel,
        grid=(blocks,),
        in_specs=[pl.BlockSpec((1, share, n), lambda block: (block, 0, 0))] * 8,
        out_specs=pl.BlockSpec((1, 4, share, 2 * n), lambda block: (block, 0, 0, 0)),
        out_shape=jax.ShapeDtypeStruct((blocks, 4, share, 2 * n), low),
        name="assemble_units",
    )(*parts)
    return whole.reshape(4 * blocks * share, 2 * n)


def assemble_square(parts):
    width, n = parts[0].shape[1:]
    heads, deep = width // HD, HD // 4

    def kernel(*refs):
        qkv_ref, out_ref = refs[8:]
        for at in range(8):
            lanes = pl.ds((at // 4) * n, n)
            for head in range(heads):
                for kind in range(3):
                    rows = pl.ds((kind * heads + head) * deep, deep)
                    qkv_ref[0, kind, 0, head, at % 4, :, lanes] = refs[at][0, rows]
                rows = pl.ds((3 * heads + head) * deep, deep)
                out_ref[0, head, at % 4, :, lanes] = refs[at][0, rows]

    qkv, out = pl.pallas_call(
        kernel,
        grid=(4,),
        in_specs=[pl.BlockSpec((1, width, n), lambda block: (block, 0, 0))] * 8,
        out_specs=[
            pl.BlockSpec((1, 3, 1, heads, 4, deep, 2 * n), lambda block: (block // 2, 0, block % 2, 0, 0, 0, 0)),
            pl.BlockSpec((1, heads, 4, deep, 2 * n), lambda block: (block, 0, 0, 0, 0)),
        ],
        out_shape=[
            jax.ShapeDtypeStruct((2, 3, 2, heads, 4, deep, 2 * n), low),
            jax.ShapeDtypeStruct((4, heads, 4, deep, 2 * n), low),
        ],
        name="assemble_square",
    )(*parts)
    return qkv.reshape(12 * width, 2 * n), out.reshape(4 * width, 2 * n)


def scaled_product(slope, weight, rows):
    units, full = weight.shape
    tokens = rows.shape[1]
    step = 512 if units % 512 == 0 else units

    def kernel(slope_ref, weight_ref, rows_ref, out_ref, sum_ref):
        product = dot_nn(weight_ref[...], rows_ref[...])
        product = (slope_ref[...].astype(jnp.float32) * product).astype(low)
        out_ref[...] = product
        sum_ref[...] = jnp.sum(product.astype(jnp.float32), axis=1, keepdims=True)

    return pl.pallas_call(
        kernel,
        grid=(units // step,),
        in_specs=[
            pl.BlockSpec((step, tokens), lambda at: (at, 0)),
            pl.BlockSpec((step, full), lambda at: (at, 0)),
            pl.BlockSpec((full, tokens), lambda at: (0, 0)),
        ],
        out_specs=[
            pl.BlockSpec((step, tokens), lambda at: (at, 0)),
            pl.BlockSpec((step, 1), lambda at: (at, 0)),
        ],
        out_shape=(
            jax.ShapeDtypeStruct((units, tokens), low),
            jax.ShapeDtypeStruct((units, 1), jnp.float32),
        ),
        cost_estimate=pl.CostEstimate(
            flops=2 * units * full * tokens,
            bytes_accessed=4 * units * tokens + 2 * units * full,
            transcendentals=0,
        ),
        name="scaled_product",
    )(slope, weight, rows)


def plane_steps(keep, send):
    keep, send = yield [keep, send]
    (got,) = yield [swap(send, "row", 1)]
    parts = [add(keep[:, at], got[:, at]) for at in range(4)]
    got = yield [swap(parts[at], "seqs", at) for at in (1, 2, 3)]
    return add(parts[0], *got)


def far_steps(keep, send):
    blocks = yield from plane_steps(keep, send)
    (got,) = yield [swap(blocks, "col", 2)]
    return got


def end_steps(own, far):
    (got,) = yield [swap(add(own[1], far[1]), "col", 1)]
    near = add(own[0], far[0], got)
    return by_place(jnp.stack([near] + (yield [swap(near, "seqs", at) for at in (1, 2, 3)])), "seqs")


def reduce_steps(keep, send):
    blocks = yield from plane_steps(keep, send)
    (far,) = yield [swap(blocks[2:], "col", 2)]
    return (yield from end_steps(blocks[:2], far))


def near_steps(keep, send, far):
    own = yield from plane_steps(keep, send)
    return (yield from end_steps(own, far.result))


def sum_steps(array):
    (array,) = yield [array]
    (got,) = yield [swap(array, "row", 1)]
    array = array + got
    array = sum((yield [swap(array, "seqs", at) for at in (1, 2, 3)]), array)
    return sum((yield [swap(array[at], "col", at) for at in (1, 2, 3)]), array[0])


class Chain:
    def __init__(self, steps):
        self.steps, self.result = steps, None
        self.flight = next(steps)

    def advance(self, flight):
        try:
            self.flight = self.steps.send(flight)
        except StopIteration as stop:
            self.flight, self.result = [], stop.value


def stage(main, *chains):
    chains = [chain for chain in chains if chain.result is None]
    main, flights = lax.optimization_barrier((main, [chain.flight for chain in chains]))
    for chain, flight in zip(chains, flights):
        chain.advance(flight)
    return main


def drain(*chains):
    while any(chain.result is None for chain in chains):
        stage(jnp.zeros((), jnp.float32), *chains)


def gelu_both(pre):
    size = jnp.abs(pre)
    bell = jnp.exp(-0.5 * (pre * pre))
    t = 1.0 / (1.0 + (0.3275911 * math.sqrt(0.5)) * size)
    tail = 0.5 * 1.061405429
    for term in (-1.453152027, 1.421413741, -0.284496736, 0.254829592):
        tail = tail * t + 0.5 * term
    tail = tail * t * bell
    phi = jnp.where(pre < 0.0, tail, 1.0 - tail)
    return pre * phi, phi + pre * bell * (1.0 / math.sqrt(2.0 * math.pi))


def local_fast(
    tokens,
    length,
    query_weight,
    query_bias,
    key_weight,
    value_weight,
    value_bias,
    out_weight,
    out_bias,
    first_gain,
    first_shift,
    up_weight,
    up_bias,
    down_weight,
    down_bias,
    second_gain,
    second_shift,
    cotangent,
):
    seq_count, width, slots = tokens.shape
    half = 2 * width
    full, count = 4 * width, 2 * slots
    units = up_weight.shape[1]
    row_at, col_at = lax.axis_index("row"), lax.axis_index("col")

    def turn(array):
        return jnp.where(row_at == 1, jnp.concatenate([array[half:], array[:half]], axis=0), array)

    def enter(array):
        array = lax.all_to_all(array, ("col", "row"), split_axis=0, concat_axis=0, tiled=True)
        array = array.reshape(4, 2, width, slots)
        array = jnp.concatenate([array[:, 0], array[:, 1]], axis=2)
        return turn(array.reshape(full, count))

    def arrange(array):
        array = turn(array).reshape(4, width, count)
        array = jnp.stack([array[:, :, :slots], array[:, :, slots:]], axis=1)
        return array.reshape(seq_count, width, slots)

    def leave(array):
        return lax.all_to_all(array, ("col", "row"), split_axis=0, concat_axis=0, tiled=True)

    def head_order(array):
        array = array.reshape(4, width // HD, 4, HD // 4, -1)
        return jnp.moveaxis(by_place(jnp.moveaxis(array, 2, 0), "seqs"), 0, 2).reshape(full, -1)

    def unit_order(array):
        array = array.reshape(4, 4, units // 4)
        return jnp.moveaxis(by_place(jnp.moveaxis(array, 1, 0), "seqs"), 0, 1).reshape(4 * units, 1)

    heads = width // HD
    square = [query_weight.T, key_weight.T, value_weight.T, out_weight]
    square = jnp.stack(square).astype(low).reshape(4, heads, 4, HD // 4, half)
    square = jnp.transpose(square, (2, 0, 1, 3, 4)).reshape(4, width, half)
    square = Chain(fetch_steps(square))
    up = Chain(fetch_steps(up_weight.T.astype(low).reshape(4, units // 4, half)))
    down = Chain(fetch_steps(down_weight.T.astype(low).reshape(4, units // 4, half)))

    small = [query_bias, value_bias, out_bias, first_gain, first_shift, down_bias, second_gain, second_shift]
    small = jnp.concatenate(small + [up_bias])
    small = stage(small, square)
    got = [swap(small, "col", at) for at in (1, 2, 3)]
    tokens, got = stage((tokens, got), square)
    x_low = enter(tokens)
    small = jnp.stack([small] + got)
    vectors = jnp.transpose(small[:, : 8 * width].reshape(4, 8, width), (0, 2, 1))
    bias = head_order(vectors[:, :, :2]).reshape(2, 2 * width, 2)
    bias = jnp.stack([bias[:, :, 0], jnp.zeros_like(bias[:, :, 0]), bias[:, :, 1]], axis=1).reshape(3 * full, 1)
    vectors = turn(by_place(vectors[:, :, 2:], "col").reshape(full, 6))
    vectors = [vectors[:, at : at + 1] for at in range(6)]
    ub = unit_order(small[:, 8 * width :])
    bias, vectors, ub = stage((bias, vectors, ub), square)
    stage((), square)
    qkv_full, out_full = assemble_square(square.result)
    x_low, qkv_full, out_full, bias, vectors, ub = stage((x_low, qkv_full, out_full, bias, vectors, ub), up)
    ob, gain1, shift1, db, gain2, shift2 = vectors

    qkv = (dot_nn(qkv_full, x_low) + bias).astype(low)
    mixed, lse = None, []
    for at, chains in enumerate(((), (up, down), (), (up, down))):
        if at == 3:
            qkv, mixed, cotangent = stage((qkv, mixed, cotangent), *chains)
        else:
            qkv, mixed = stage((qkv, mixed), *chains)
        mixed, part = piece_attend(length, qkv, mixed, at)
        lse.append(part)
    g = lax.optimization_barrier(enter(cotangent))
    mixed = stage(mixed, up)
    h1 = x_low.astype(jnp.float32) + (dot_tn(out_full, mixed) + ob)
    y1, n1, inv1 = normalize(h1, gain1, shift1)
    y1_low = stage(y1.astype(low), down)
    up_full = assemble_units(up.result)
    act, slope = gelu_both(dot_nn(up_full, y1_low) + ub)
    act_low, slope = stage((act.astype(low), slope.astype(low)), down)
    down_full = assemble_units(down.result)
    h2 = y1 + (dot_tn(down_full, act_low) + db)
    out, n2, inv2 = normalize(h2, gain2, shift2)
    layer_output = leave(arrange(out.astype(low)))

    ones = jnp.ones((count, 128), low)
    token_sum = lambda array: dot_nn(array, ones)[:, 0]
    valid = (jnp.arange(count, dtype=jnp.int32)[None, :] < length[:, None]).astype(jnp.float32)
    g = g.astype(jnp.float32) * valid
    gain2_grad = jnp.sum(g * n2, axis=1)
    shift2_grad = jnp.sum(g, axis=1)
    dh2 = norm_back(g, n2, inv2, gain2)
    dz = dh2.astype(low)
    db_grad = token_sum(dz)
    by_share = lambda grad: grad.astype(low).reshape(4, 4, units // 4, half)

    def halves(one, two):
        return by_share(dot_nt(one, two[:half])), by_share(dot_nt(one, two[half:]))

    down_grad = Chain(reduce_steps(*halves(act_low, dz)))
    dz = stage(dz, down_grad)
    dpre, ub_grad = scaled_product(slope, down_full, dz)
    dpre = stage(dpre, down_grad)
    up_grad = Chain(reduce_steps(*halves(dpre, y1_low)))
    dpre = stage(dpre, up_grad)
    dy1 = dh2 + dot_tn(up_full, dpre)
    gain1_grad = jnp.sum(dy1 * n1, axis=1)
    shift1_grad = jnp.sum(dy1, axis=1)
    dh1 = norm_back(dy1, n1, inv1, gain1)
    da = dh1.astype(low)
    da = stage(da)
    ob_grad = token_sum(da)
    out_grad = [dot_nt(mixed, part).astype(low) for part in (da[:half], da[half:])]
    grad_mixed = dot_nn(out_full, da).astype(low)
    grad_mixed, out_grad = stage((grad_mixed, out_grad), up_grad)

    def square_share(pair, dqkv):
        rows = dqkv.reshape(6 * width, count)
        shares = []
        for part, other in zip((x_low[:half], x_low[half:]), out_grad):
            grad = dot_nt(rows, part).astype(low).reshape(3, 2 * width, half)
            other = other[2 * width * pair : 2 * width * (pair + 1)]
            grad = jnp.concatenate([grad, other[None]], axis=0).reshape(4, 2, heads, 4, HD // 4, half)
            shares.append(jnp.transpose(grad, (1, 3, 0, 2, 4, 5)).reshape(2, 4, width, half))
        return shares

    dqkv = piece_attend_back(length, qkv, mixed, lse[2], grad_mixed, None, 2)
    grad_mixed, dqkv = stage((grad_mixed, dqkv), down_grad)
    dqkv = piece_attend_back(length, qkv, mixed, lse[3], grad_mixed, dqkv, 3)
    grad_mixed, dqkv, layer_output = stage((grad_mixed, dqkv, layer_output), down_grad)
    far = Chain(far_steps(*square_share(1, dqkv)))
    dx = dh1 + dot_tn(qkv_full[6 * width :], dqkv.reshape(6 * width, count))
    v_sums = [token_sum(dqkv[2])]
    q_sums = [token_sum(dqkv[0])]
    by_col = lambda parts: jnp.transpose(jnp.concatenate(parts, axis=1).reshape(4, width, -1), (0, 2, 1))
    vectors = turn(jnp.stack([ob_grad, gain1_grad, shift1_grad, db_grad, gain2_grad, shift2_grad], axis=1))
    vectors = by_col([by_place(vectors.reshape(4, width, 6), "col").reshape(full, 6)]).reshape(4, 6 * width)
    ub_grad = unit_order(ub_grad.reshape(4, units)).reshape(4, units)
    early = jnp.concatenate([vectors, ub_grad], axis=1)
    grad_mixed, dx, v_sums, q_sums, early = stage(
        (grad_mixed, dx, v_sums, q_sums, early), far, up_grad, down_grad
    )
    dqkv = piece_attend_back(length, qkv, mixed, lse[0], grad_mixed, None, 0)
    grad_mixed, dqkv = stage((grad_mixed, dqkv), far, up_grad)
    dqkv = piece_attend_back(length, qkv, mixed, lse[1], grad_mixed, dqkv, 1)
    dqkv = stage(dqkv, up_grad, down_grad)
    square_grad = Chain(near_steps(*square_share(0, dqkv), far))
    dqkv, dx = stage((dqkv, dx), square_grad, far)
    dx = dx + dot_tn(qkv_full[: 6 * width], dqkv.reshape(6 * width, count))
    dx, dqkv = stage((arrange(dx.astype(low)), dqkv), square_grad, far, up_grad)
    tokens_grad = leave(dx)
    v_sums = jnp.concatenate([token_sum(dqkv[2])] + v_sums)
    q_sums = jnp.concatenate([token_sum(dqkv[0])] + q_sums)
    late = head_order(jnp.stack([q_sums, v_sums], axis=1).reshape(4, width, 2))
    late = by_col([late]).reshape(4, 2 * width)
    small_grad = Chain(sum_steps(jnp.concatenate([late, early], axis=1)))
    drain(square_grad, far, up_grad, small_grad)

    small_grad = small_grad.result
    pieces = [small_grad[at * width : (at + 1) * width] for at in range(8)]
    square_grad = square_grad.result.reshape(4, 4, heads, HD // 4, half)
    square_grad = jnp.transpose(square_grad, (1, 2, 0, 3, 4)).reshape(4, width, half).astype(jnp.float32)
    block = lambda grad: grad.result.reshape(units, half).astype(jnp.float32).T
    return (
        layer_output,
        tokens_grad,
        square_grad[0].T,
        pieces[0],
        square_grad[1].T,
        square_grad[2].T,
        pieces[1],
        square_grad[3],
        pieces[2],
        pieces[3],
        pieces[4],
        block(up_grad),
        small_grad[8 * width :],
        block(down_grad),
        pieces[5],
        pieces[6],
        pieces[7],
    )


def local(
    tokens,
    lengths,
    query_weight,
    query_bias,
    key_weight,
    value_weight,
    value_bias,
    out_weight,
    out_bias,
    first_gain,
    first_shift,
    up_weight,
    up_bias,
    down_weight,
    down_bias,
    second_gain,
    second_shift,
    cotangent,
):
    seq_count, width, rows = tokens.shape
    row, col = lax.axis_size("row"), lax.axis_size("col")
    row_at, col_at = lax.axis_index("row"), lax.axis_index("col")
    members = row * col
    full = width * col
    alone = seq_count % members == 0
    if alone:
        count = seq_count // members
        mine = row * rows
        first = jnp.int32(0)
        own_lengths = lax.dynamic_slice_in_dim(lengths, (col_at * row + row_at) * count, count, 0)
    else:
        count = seq_count // col
        mine = rows
        first = row_at * rows
        own_lengths = lax.dynamic_slice_in_dim(lengths, col_at * count, count, 0)

    def enter(array):
        if alone:
            array = lax.all_to_all(array, ("col", "row"), split_axis=0, concat_axis=0, tiled=True)
            array = array.reshape(col, row, count, width, rows)
            return jnp.transpose(array, (0, 3, 2, 1, 4)).reshape(full, count * mine)
        array = lax.all_to_all(array, "col", split_axis=0, concat_axis=0, tiled=True)
        array = array.reshape(col, count, width, rows)
        return jnp.transpose(array, (0, 2, 1, 3)).reshape(full, count * mine)

    def leave(array):
        if alone:
            array = array.reshape(col, width, count, row, rows)
            array = jnp.transpose(array, (0, 3, 2, 1, 4)).reshape(seq_count, width, rows)
            return lax.all_to_all(array, ("col", "row"), split_axis=0, concat_axis=0, tiled=True)
        array = jnp.transpose(array.reshape(col, width, count, mine), (0, 2, 1, 3))
        array = array.reshape(seq_count, width, rows)
        return lax.all_to_all(array, "col", split_axis=0, concat_axis=0, tiled=True)

    if alone and lax.axis_size("seqs") == 4 and row == 2 and col == 4 and count == 1 and width == 3 * HD:
        return local_fast(
            tokens,
            own_lengths,
            query_weight,
            query_bias,
            key_weight,
            value_weight,
            value_bias,
            out_weight,
            out_bias,
            first_gain,
            first_shift,
            up_weight,
            up_bias,
            down_weight,
            down_bias,
            second_gain,
            second_shift,
            cotangent,
        )

    def by_sequence(move, array):
        parts = [move(part) for part in jnp.split(array, count, axis=1)]
        return jnp.concatenate(parts, axis=1)

    def all_keys(array):
        if alone:
            return array
        return by_sequence(lambda part: lax.all_gather(part, "row", axis=1, tiled=True), array)

    def own_keys(array):
        if alone:
            return array
        return by_sequence(
            lambda part: lax.psum_scatter(part, "row", scatter_dimension=1, tiled=True), array
        )

    x_low = enter(tokens)
    qkv_piece = jnp.concatenate([query_weight, key_weight, value_weight], axis=1).astype(low)
    qkv_full = spread(qkv_piece)
    out_full = spread(out_weight.T.astype(low))
    up_full = spread(up_weight.astype(low))
    down_full = spread(down_weight.astype(low))
    small = jnp.concatenate(
        [
            query_bias,
            value_bias,
            out_bias,
            first_gain,
            first_shift,
            down_bias,
            second_gain,
            second_shift,
            up_bias,
        ]
    )
    small = lax.all_gather(small, "col", axis=0, tiled=False)
    vectors = [small[:, at * width : (at + 1) * width].reshape(full, 1) for at in range(8)]
    qb, vb, ob, gain1, shift1, db, gain2, shift2 = vectors
    ub = small[:, 8 * width :].reshape(-1, 1)

    token_count = count * mine
    qkv = up_form(qkv_full, x_low).reshape(col, 3, width, token_count)
    q = (qkv[:, 0].reshape(full, token_count) + qb).astype(low)
    k = qkv[:, 1].reshape(full, token_count).astype(low)
    v = (qkv[:, 2].reshape(full, token_count) + vb).astype(low)
    k_all, v_all = all_keys(k), all_keys(v)
    mixed, lse = attention(own_lengths, q, k_all, v_all, count)
    h1 = x_low.astype(jnp.float32) + (down_form(out_full, mixed) + ob)
    y1, n1, inv1 = normalize(h1, gain1, shift1)
    y1_low = y1.astype(low)
    pre = up_form(up_full, y1_low) + ub
    act, gelu_back = jax.vjp(partial(jax.nn.gelu, approximate=False), pre)
    act_low = act.astype(low)
    h2 = y1 + (down_form(down_full, act_low) + db)
    out, n2, inv2 = normalize(h2, gain2, shift2)
    layer_output = leave(out.astype(low))

    position = first + jnp.arange(mine, dtype=jnp.int32)
    valid = (position[None, :] < own_lengths[:, None]).astype(jnp.float32).reshape(1, token_count)
    g = enter(cotangent).astype(jnp.float32) * valid
    gain2_grad = jnp.sum(g * n2, axis=1)
    shift2_grad = jnp.sum(g, axis=1)
    dh2 = norm_back(g, n2, inv2, gain2)
    dz = dh2.astype(low)
    db_grad = jnp.sum(dz, axis=1, dtype=jnp.float32)
    down_grad = collect(dot_nt(dz, act_low))
    dpre = gelu_back(up_form(down_full, dz))[0].astype(low)
    ub_grad = jnp.sum(dpre, axis=1, dtype=jnp.float32)
    up_grad = collect(dot_nt(y1_low, dpre))
    dy1 = dh2 + down_form(up_full, dpre)
    gain1_grad = jnp.sum(dy1 * n1, axis=1)
    shift1_grad = jnp.sum(dy1, axis=1)
    dh1 = norm_back(dy1, n1, inv1, gain1)
    da = dh1.astype(low)
    ob_grad = jnp.sum(da, axis=1, dtype=jnp.float32)
    out_grad = collect(dot_nt(da, mixed))
    grad_mixed = up_form(out_full, da).astype(low)
    dq, dk, dv = attention_back(own_lengths, q, k_all, v_all, mixed, lse, grad_mixed, count)
    dk, dv = own_keys(dk), own_keys(dv)
    qb_grad = jnp.sum(dq, axis=1, dtype=jnp.float32)
    vb_grad = jnp.sum(dv, axis=1, dtype=jnp.float32)
    block = lambda array: array.reshape(col, width, token_count)
    dqkv = jnp.stack([block(dq), block(dk), block(dv)], axis=1).reshape(3 * full, token_count)
    dx = dh1 + down_form(qkv_full, dqkv)
    tokens_grad = leave(dx.astype(low))
    qkv_grad = collect(dot_nt(x_low, dqkv)).astype(jnp.float32)
    vectors = [qb_grad, vb_grad, ob_grad, gain1_grad, shift1_grad, db_grad, gain2_grad, shift2_grad]
    vectors = [vector.reshape(col, width) for vector in vectors] + [ub_grad.reshape(col, -1)]
    small_grad = lax.psum(jnp.concatenate(vectors, axis=1), ("seqs", "row", "col"))
    small_grad = lax.dynamic_index_in_dim(small_grad, col_at, 0, keepdims=False)
    pieces = [small_grad[at * width : (at + 1) * width] for at in range(8)]
    return (
        layer_output,
        tokens_grad,
        qkv_grad[:, :width],
        pieces[0],
        qkv_grad[:, width : 2 * width],
        qkv_grad[:, 2 * width :],
        pieces[1],
        out_grad.astype(jnp.float32).T,
        pieces[2],
        pieces[3],
        pieces[4],
        up_grad.astype(jnp.float32),
        small_grad[8 * width :],
        down_grad.astype(jnp.float32),
        pieces[5],
        pieces[6],
        pieces[7],
    )


def solution(mesh):
    wide, vector = P("seqs", "col", "row"), P("col")
    square, turned = P("row", "col"), P("col", "row")
    in_specs = (
        wide,
        P("seqs"),
        square,
        vector,
        square,
        square,
        vector,
        turned,
        vector,
        vector,
        vector,
        square,
        vector,
        square,
        vector,
        vector,
        vector,
        wide,
    )
    out_specs = (
        wide,
        wide,
        square,
        vector,
        square,
        square,
        vector,
        turned,
        vector,
        vector,
        vector,
        square,
        vector,
        square,
        vector,
        vector,
        vector,
    )
    return jax.shard_map(local, mesh=mesh, in_specs=in_specs, out_specs=out_specs, check_vma=False)
```
